256 devices in a mesh: grp: 8 (over y_hi, x), blk: 32 (over z, y_lo, core).
Axes of the slice: x: 4, y: 4 (y_hi: 2, y_lo: 2; y = y_hi * 2 + y_lo), z: 8, core: 2. Of those that a mesh axis runs over, the one named last changes fastest.
Arguments:
- tokens: bfloat16 [16384, 4096], P(('blk', 'grp')), may hold values from -16 to 16
- w_query: bfloat16 [4096, 4096], P(None, 'grp'), may hold values from -0.09375 to 0.09375
- key_weight: bfloat16 [4096, 1024], P(None, 'grp'), may hold values from -0.09375 to 0.09375
- value_weight: bfloat16 [4096, 1024], P(None, 'grp'), may hold values from -0.09375 to 0.09375
- w_output: bfloat16 [4096, 4096], P('grp'), may hold values from -0.09375 to 0.09375
- block_mask: int32 [128, 128], P('blk'), may hold values from 0 to 1, as said below
- positions: int32 [16384], P('blk'), may hold values from 0 to 98301, as said below
Outputs:
- attended: bfloat16 [16384, 4096], P(('blk', 'grp'))
The draws below stay inside these ranges and needn't reach their ends.
Inputs may be any that keep to these rules, and one draw needn't show every extreme that they name: block_mask[i, j] is 1 exactly where |i - j| <= 1, where i < 1 or j < 1, or where j is one of 3 distinct blocks drawn for row i; so query blocks below 1 attend every key block. A sequence block is a run of 512 tokens from a multiple of 512. The drawn blocks of a row never lie in its own sequence block, in the two sequence blocks beside it (the last and the first count as beside each other) or in the first sequence block. Over the query blocks of one sequence block, other than those below 1, the live key blocks that lie outside that sequence block, are not the block just before or just after it, and are not below 1, number at most 1 in any one other sequence block. positions rise along the sequence by 1 or 2 per token; the last token's position is the most.
All inputs are finite; a program needn't handle non-finite values.
Results may differ from the reference program's by a relative error of at most 0.017.
Values may be sent and summed in bfloat16 or wider, within the bound.
A program may use at most 64 MiB of HBM per device.

```python
import jax
import jax.numpy as jnp
from jax import lax

MODEL_WIDTH = 4096
QUERY_HEADS = 32
KEY_VALUE_HEADS = 8
HEAD_WIDTH = 128
MASK_BLOCK_TOKENS = 128
GLOB = 1
RAND = 3
SEQUENCE_TOKENS = 16384
MASK_BLOCK_COUNT = 128
ROWS = 512
N_GRP = 8


def draw_tokens(key, part):
    return jnp.clip(jax.random.normal(jax.random.fold_in(key, 31), (SEQUENCE_TOKENS, MODEL_WIDTH), jnp.float32), -6.0, 6.0).astype(jnp.bfloat16)


def pick_blocks(base_key, owner):
    per_device = ROWS // MASK_BLOCK_TOKENS
    owners = SEQUENCE_TOKENS // ROWS
    eligible = owners - 4
    owner_key = jax.random.fold_in(base_key, owner)
    order = jax.random.permutation(jax.random.fold_in(owner_key, 1), owners).astype(jnp.int32)
    excluded = (order == owner) | (order == (owner + 1) % owners) | (order == (owner + owners - 1) % owners) | (order == 0)
    ranking = excluded.astype(jnp.int32) * owners + jnp.arange(owners, dtype=jnp.int32)
    chosen = order[jnp.argsort(ranking)]
    offset_base = jax.random.randint(jax.random.fold_in(owner_key, 2), (owners,), 0, per_device)
    pick_ids = jnp.arange(per_device * RAND, dtype=jnp.int32)
    target = chosen[pick_ids % eligible]
    offset = (offset_base[target] + pick_ids // eligible) % per_device
    return (target * per_device + offset).reshape(per_device, RAND)


def draw_block_mask(key, part):
    count = SEQUENCE_TOKENS // MASK_BLOCK_TOKENS
    owners = SEQUENCE_TOKENS // ROWS
    row_ids = jnp.arange(count)[:, None]
    col_ids = jnp.arange(count)[None, :]
    band = jnp.abs(row_ids - col_ids) <= 1
    global_part = (row_ids < GLOB) | (col_ids < GLOB)
    base_key = jax.random.fold_in(key, 11)
    picks = jax.vmap(lambda owner: pick_blocks(base_key, owner))(jnp.arange(owners, dtype=jnp.int32)).reshape(count, RAND)
    random_part = jnp.any(picks[:, :, None] == jnp.arange(count)[None, None, :], axis=1)
    return (band | global_part | random_part).astype(jnp.int32)


def draw_positions(key, part):
    second_key = jax.random.fold_in(key, 22)
    steps_drawn = jax.random.randint(second_key, (SEQUENCE_TOKENS,), 1, 3).astype(jnp.int32)
    last_position = 65535 + 2 * (SEQUENCE_TOKENS - 1)
    after = jnp.cumsum(steps_drawn[::-1])[::-1] - steps_drawn
    return (last_position - after).astype(jnp.int32)


def levels(own_key, dims, pieces, low, top_value):
    factor_of, own = 1.0, jax.random.fold_in(own_key, 6)
    for axis_at, shards_of in pieces:
        heights = jnp.exp(jax.random.uniform(jax.random.fold_in(own, axis_at), (shards_of,), jnp.float32, low / len(pieces), top_value / len(pieces)))
        factor_of = factor_of * jnp.repeat(heights, dims[axis_at] // shards_of).reshape([-1 if axis == axis_at else 1 for axis in range(len(dims))])
    return factor_of


def scatter_about(own_key, dims, scale, reach, split=(), kind=jnp.bfloat16):
    level = levels(own_key, dims, split, -0.22, 0.18) if split else 1.0
    drawn = jax.random.normal(own_key, dims, jnp.float32) * scale * level
    return jnp.minimum(jnp.maximum(drawn, -reach), reach).astype(kind)


def setup_inputs(seed: int = 0) -> dict:
    splits = jax.random.split(jax.random.key(seed), 8)
    return {
        "tokens": draw_tokens(jax.random.fold_in(splits[7], 71), 0),
        "w_query": scatter_about(splits[1], (MODEL_WIDTH, QUERY_HEADS * HEAD_WIDTH), MODEL_WIDTH ** -0.5, 0.09375, ((1, 8),)),
        "key_weight": scatter_about(splits[2], (MODEL_WIDTH, KEY_VALUE_HEADS * HEAD_WIDTH), MODEL_WIDTH ** -0.5, 0.09375, ((1, 8),)),
        "value_weight": scatter_about(splits[3], (MODEL_WIDTH, KEY_VALUE_HEADS * HEAD_WIDTH), MODEL_WIDTH ** -0.5, 0.09375, ((1, 8),)),
        "w_output": scatter_about(splits[4], (QUERY_HEADS * HEAD_WIDTH, MODEL_WIDTH), (QUERY_HEADS * HEAD_WIDTH) ** -0.5, 0.09375, ((0, 8),)),
        "block_mask": draw_block_mask(jax.random.fold_in(splits[7], 71), 0),
        "positions": draw_positions(jax.random.fold_in(splits[7], 71), 0),
    }


NEG_FILL = -1e30


def rotary_position(projected, positions, heads):
    half = HEAD_WIDTH // 2
    inverse = jnp.power(jnp.float32(500000.0), -(2.0 * jnp.arange(half, dtype=jnp.float32)) / HEAD_WIDTH)
    angles = positions.astype(jnp.float32)[:, None] * inverse[None, :]
    cosine = jnp.cos(angles)[:, None, :]
    sine = jnp.sin(angles)[:, None, :]
    shaped = projected.reshape(projected.shape[0], heads, HEAD_WIDTH)
    first = shaped[..., :half]
    second = shaped[..., half:]
    turned = jnp.concatenate([first * cosine - second * sine, second * cosine + first * sine], axis=-1)
    return turned.reshape(projected.shape[0], heads * HEAD_WIDTH)


def reference(tokens, w_query, key_weight, value_weight, w_output, block_mask, positions):
    query_rows = rotary_position(jnp.dot(tokens, w_query, preferred_element_type=jnp.float32), positions, QUERY_HEADS).astype(jnp.bfloat16)
    key_rows = rotary_position(jnp.dot(tokens, key_weight, preferred_element_type=jnp.float32), positions, KEY_VALUE_HEADS).astype(jnp.bfloat16)
    value_rows = jnp.dot(tokens, value_weight, preferred_element_type=jnp.float32).astype(jnp.bfloat16)
    head_repeat_count = QUERY_HEADS // KEY_VALUE_HEADS
    scale = HEAD_WIDTH ** -0.5
    key_single_precision = key_rows.astype(jnp.float32).reshape(SEQUENCE_TOKENS, KEY_VALUE_HEADS, HEAD_WIDTH)
    value_single_precision = value_rows.astype(jnp.float32).reshape(SEQUENCE_TOKENS, KEY_VALUE_HEADS, HEAD_WIDTH)
    query_block_rows = query_rows.reshape(MASK_BLOCK_COUNT, MASK_BLOCK_TOKENS, KEY_VALUE_HEADS, head_repeat_count, HEAD_WIDTH)

    def one_block(item):
        block_query, row_mask = item
        scores = jnp.einsum('qcrd,kcd->crqk', block_query.astype(jnp.float32), key_single_precision) * scale
        live = jnp.repeat(row_mask != 0, MASK_BLOCK_TOKENS)[None, None, None, :]
        scores = jnp.where(live, scores, NEG_FILL)
        top = jnp.max(scores, axis=-1, keepdims=True)
        weights = jnp.where(live, jnp.exp(scores - top), 0.0)
        total = jnp.sum(weights, axis=-1)
        rounded = lax.optimization_barrier(weights.astype(jnp.bfloat16)).astype(jnp.float32)
        mixed = jnp.einsum('crqk,kcd->crqd', rounded, value_single_precision) / total[..., None]
        return mixed.transpose(2, 0, 1, 3).reshape(MASK_BLOCK_TOKENS, QUERY_HEADS * HEAD_WIDTH).astype(jnp.bfloat16)

    mixed_all = lax.map(one_block, (query_block_rows, block_mask)).reshape(SEQUENCE_TOKENS, QUERY_HEADS * HEAD_WIDTH)
    width = QUERY_HEADS * HEAD_WIDTH // N_GRP
    result = jnp.zeros((SEQUENCE_TOKENS, MODEL_WIDTH), jnp.float32)
    for group in range(N_GRP):
        partial_sum = jnp.dot(mixed_all[:, group * width:(group + 1) * width], w_output[group * width:(group + 1) * width], preferred_element_type=jnp.float32)
        result = result + lax.optimization_barrier(partial_sum.astype(jnp.bfloat16)).astype(jnp.float32)
    return result.astype(jnp.bfloat16)
```

```python
import functools

import jax
import jax.numpy as jnp
from jax import lax
from jax.experimental import pallas as pl
from jax.experimental.pallas import tpu as pltpu
from jax.sharding import PartitionSpec as P

HEAD = 128
BLOCK = 128
NEG = -1e30
LOG2E = 1.4426950408889634
SCALE2 = HEAD ** (-0.5) * LOG2E


def rotary_tables(positions):
    half = HEAD // 2
    inverse = jnp.power(
        jnp.float32(500000.0), -(2.0 * jnp.arange(half, dtype=jnp.float32)) / HEAD
    )
    angles = positions.astype(jnp.float32)[:, None] * inverse[None, :]
    cosine, sine = jnp.cos(angles), jnp.sin(angles)
    return (
        jnp.concatenate([cosine, cosine], axis=1),
        jnp.concatenate([-sine, sine], axis=1),
    )


def turn(v, cosine, sine):
    return v * cosine + pltpu.roll(v, HEAD // 2, 1) * sine


def project_kernel(x_ref, wq_ref, wk_ref, wv_ref, cos_ref, sin_ref, q_ref, kv_ref):
    cosine, sine = cos_ref[...], sin_ref[...]
    x = x_ref[...]
    k = jnp.dot(x, wk_ref[...], preferred_element_type=jnp.float32)
    kv_ref[:, :HEAD] = turn(k, cosine, sine).astype(jnp.bfloat16)
    v = jnp.dot(x, wv_ref[...], preferred_element_type=jnp.float32)
    kv_ref[:, HEAD:] = v.astype(jnp.bfloat16)
    q = jnp.dot(x, wq_ref[...], preferred_element_type=jnp.float32)
    for h in range(wq_ref.shape[1] // HEAD):
        cols = slice(h * HEAD, (h + 1) * HEAD)
        q_ref[:, cols] = turn(q[:, cols], cosine, sine).astype(jnp.bfloat16)


def project(piece, wq, wk, wv, cosine, sine):
    rows = piece.shape[0]
    step = 128
    return pl.pallas_call(
        project_kernel,
        grid=(rows // step,),
        in_specs=[
            pl.BlockSpec((step, piece.shape[1]), lambda i: (i, 0)),
            pl.BlockSpec(wq.shape, lambda i: (0, 0)),
            pl.BlockSpec(wk.shape, lambda i: (0, 0)),
            pl.BlockSpec(wv.shape, lambda i: (0, 0)),
            pl.BlockSpec((step, HEAD), lambda i: (i, 0)),
            pl.BlockSpec((step, HEAD), lambda i: (i, 0)),
        ],
        out_specs=[
            pl.BlockSpec((step, wq.shape[1]), lambda i: (i, 0)),
            pl.BlockSpec((step, 2 * HEAD), lambda i: (i, 0)),
        ],
        out_shape=[
            jax.ShapeDtypeStruct((rows, wq.shape[1]), jnp.bfloat16),
            jax.ShapeDtypeStruct((rows, 2 * HEAD), jnp.bfloat16),
        ],
    )(piece, wq, wk, wv, cosine, sine)


def score(q, k):
    return lax.dot_general(q, k, (((1,), (1,)), ((), ())), preferred_element_type=jnp.float32)


def attend_kernel(
    n_blocks, chunk, heads, mask_ref, q_ref, kv_ref, out_ref, near, stream, sem, stream_sem
):
    blk = lax.axis_index("blk")
    rows = q_ref.shape[0] // BLOCK
    lanes = lax.broadcasted_iota(jnp.int32, (1, n_blocks), 1)
    copies = []
    for r in range(rows):
        i = blk * rows + r
        live = mask_ref[r : r + 1, :] != 0
        fixed = (jnp.abs(lanes - i) <= 1) | (lanes < 1)
        left = jnp.where(live & jnp.logical_not(fixed), lanes, n_blocks)
        ids = [0, jnp.maximum(i - 1, 0), i, jnp.minimum(i + 1, n_blocks - 1)]
        last = jnp.int32(-1)
        for _ in range(3):
            last = jnp.min(jnp.where(left > last, left, n_blocks))
            ids.append(jnp.minimum(last, n_blocks - 1))
        for s, j in enumerate(ids):
            copies.append(
                pltpu.make_async_copy(
                    kv_ref.at[pl.ds(pl.multiple_of(j * BLOCK, BLOCK), BLOCK)],
                    near.at[r, pl.ds(s * BLOCK, BLOCK)],
                    sem.at[r, s],
                )
            )
            copies[-1].start()
    slots = len(copies) // rows

    def queries(r):
        return jnp.concatenate(
            [
                q_ref[r * BLOCK : (r + 1) * BLOCK, h * HEAD : (h + 1) * HEAD]
                for h in range(heads)
            ],
            axis=0,
        )

    def put(r, mixed):
        for h in range(heads):
            out_ref[r * BLOCK : (r + 1) * BLOCK, h * HEAD : (h + 1) * HEAD] = mixed[
                h * BLOCK : (h + 1) * BLOCK
            ].astype(jnp.bfloat16)

    for r in range(rows):
        i = blk * rows + r
        for s in range(slots):
            copies[r * slots + s].wait()
        s = score(queries(r), near[r, :, :HEAD])
        parts = [
            jnp.where(i == 1, NEG, s[:, :BLOCK]),
            s[:, BLOCK : 3 * BLOCK],
            jnp.where(i == n_blocks - 1, NEG, s[:, 3 * BLOCK : 4 * BLOCK]),
            s[:, 4 * BLOCK :],
        ]
        s = jnp.concatenate(parts, axis=1)
        top = jnp.max(s, axis=1, keepdims=True)
        p = jnp.exp2(s * SCALE2 - top * SCALE2)
        total = jnp.sum(p, axis=1, keepdims=True)
        mixed = jnp.dot(
            p.astype(jnp.bfloat16), near[r, :, HEAD:], preferred_element_type=jnp.float32
        )
        put(r, mixed / total)

    @pl.when(blk == 0)
    def _():
        keys = chunk * BLOCK
        steps = n_blocks // chunk

        def fetch(step, slot):
            return pltpu.make_async_copy(
                kv_ref.at[pl.ds(pl.multiple_of(step * keys, keys), keys)],
                stream.at[slot],
                stream_sem.at[slot],
            )

        fetch(0, 0).start()
        q = queries(0)
        n = q.shape[0]

        def body(step, state):
            top, total, accum = state
            slot = lax.rem(step, 2)
            fetch(step, slot).wait()

            @pl.when(step + 1 < steps)
            def _():
                fetch(step + 1, 1 - slot).start()

            s = score(q, stream[slot, :, :HEAD])
            new = jnp.maximum(top, jnp.max(s, axis=1, keepdims=True))
            p = jnp.exp2(s * SCALE2 - new * SCALE2)
            factor = jnp.exp2((top - new) * SCALE2)
            total = total * factor + jnp.sum(p, axis=1, keepdims=True)
            accum = accum * factor + jnp.dot(
                p.astype(jnp.bfloat16),
                stream[slot, :, HEAD:],
                preferred_element_type=jnp.float32,
            )
            return new, total, accum

        top, total, accum = lax.fori_loop(
            0,
            steps,
            body,
            (
                jnp.full((n, 1), NEG, jnp.float32),
                jnp.zeros((n, 1), jnp.float32),
                jnp.zeros((n, HEAD), jnp.float32),
            ),
        )
        put(0, accum / total)


def attend(block_mask, q, kv):
    rows = q.shape[0] // BLOCK
    n_blocks = kv.shape[0] // BLOCK
    heads = q.shape[1] // HEAD
    chunk = 8
    vmem = pl.BlockSpec(memory_space=pltpu.VMEM)
    return pl.pallas_call(
        functools.partial(attend_kernel, n_blocks, chunk, heads),
        in_specs=[vmem, vmem, pl.BlockSpec(memory_space=pl.ANY)],
        out_specs=vmem,
        out_shape=jax.ShapeDtypeStruct(q.shape, jnp.bfloat16),
        scratch_shapes=[
            pltpu.VMEM((rows, 7 * BLOCK, 2 * HEAD), jnp.bfloat16),
            pltpu.VMEM((2, chunk * BLOCK, 2 * HEAD), jnp.bfloat16),
            pltpu.SemaphoreType.DMA((rows, 7)),
            pltpu.SemaphoreType.DMA((2,)),
        ],
    )(block_mask, q, kv)


def body(tokens, w_query, key_weight, value_weight, w_output, block_mask, positions):
    cosine, sine = rotary_tables(positions)
    piece = lax.all_gather(tokens, "grp", axis=0, tiled=True)
    q, kv = project(piece, w_query, key_weight, value_weight, cosine, sine)
    kv = lax.all_gather(kv, "blk", axis=0, tiled=True)
    mixed = attend(block_mask, q, kv)
    term = jnp.dot(mixed, w_output, preferred_element_type=jnp.float32)
    return lax.psum_scatter(
        term.astype(jnp.bfloat16), "grp", scatter_dimension=0, tiled=True
    )


def solution(mesh):
    return jax.shard_map(
        body,
        mesh=mesh,
        in_specs=(
            P(("blk", "grp"), None),
            P(None, "grp"),
            P(None, "grp"),
            P(None, "grp"),
            P("grp", None),
            P("blk", None),
            P("blk"),
        ),
        out_specs=P(("blk", "grp"), None),
        check_vma=False,
    )
```

```python
import functools

import jax
import jax.numpy as jnp
from jax import lax
from jax.experimental import pallas as pl
from jax.experimental.pallas import tpu as pltpu
from jax.sharding import PartitionSpec as P

HEAD = 128
BLOCK = 128
NEG = -1e30
LOG2E = 1.4426950408889634
SCALE2 = HEAD ** (-0.5) * LOG2E


def rotary_tables(positions):
    half = HEAD // 2
    inverse = jnp.power(
        jnp.float32(500000.0), -(2.0 * jnp.arange(half, dtype=jnp.float32)) / HEAD
    )
    angles = positions.astype(jnp.float32)[:, None] * inverse[None, :]
    cosine, sine = jnp.cos(angles), jnp.sin(angles)
    return (
        jnp.concatenate([cosine, cosine], axis=1),
        jnp.concatenate([-sine, sine], axis=1),
    )


def turn(v, cosine, sine):
    return v * cosine + pltpu.roll(v, HEAD // 2, 1) * sine


def project_kernel(x_ref, wq_ref, wk_ref, wv_ref, cos_ref, sin_ref, q_ref, kv_ref):
    cosine, sine = cos_ref[...], sin_ref[...]
    x = x_ref[...]
    k = jnp.dot(x, wk_ref[...], preferred_element_type=jnp.float32)
    kv_ref[:, :HEAD] = turn(k, cosine, sine).astype(jnp.bfloat16)
    v = jnp.dot(x, wv_ref[...], preferred_element_type=jnp.float32)
    kv_ref[:, HEAD:] = v.astype(jnp.bfloat16)
    q = jnp.dot(x, wq_ref[...], preferred_element_type=jnp.float32)
    for h in range(wq_ref.shape[1] // HEAD):
        cols = slice(h * HEAD, (h + 1) * HEAD)
        q_ref[:, cols] = turn(q[:, cols], cosine, sine).astype(jnp.bfloat16)


def project(piece, wq, wk, wv, cosine, sine):
    rows = piece.shape[0]
    step = 128
    return pl.pallas_call(
        project_kernel,
        grid=(rows // step,),
        in_specs=[
            pl.BlockSpec((step, piece.shape[1]), lambda i: (i, 0)),
            pl.BlockSpec(wq.shape, lambda i: (0, 0)),
            pl.BlockSpec(wk.shape, lambda i: (0, 0)),
            pl.BlockSpec(wv.shape, lambda i: (0, 0)),
            pl.BlockSpec((step, HEAD), lambda i: (i, 0)),
            pl.BlockSpec((step, HEAD), lambda i: (i, 0)),
        ],
        out_specs=[
            pl.BlockSpec((step, wq.shape[1]), lambda i: (i, 0)),
            pl.BlockSpec((step, 2 * HEAD), lambda i: (i, 0)),
        ],
        out_shape=[
            jax.ShapeDtypeStruct((rows, wq.shape[1]), jnp.bfloat16),
            jax.ShapeDtypeStruct((rows, 2 * HEAD), jnp.bfloat16),
        ],
    )(piece, wq, wk, wv, cosine, sine)


def score(q, k):
    return lax.dot_general(q, k, (((1,), (1,)), ((), ())), preferred_element_type=jnp.float32)


def attend_kernel(
    n_blocks, chunk, heads, mask_ref, q_ref, kv_ref, out_ref, near, stream, sem, stream_sem
):
    blk = lax.axis_index("blk")
    rows = q_ref.shape[0] // BLOCK
    lanes = lax.broadcasted_iota(jnp.int32, (1, n_blocks), 1)
    copies = []
    for r in range(rows):
        i = blk * rows + r
        live = mask_ref[r : r + 1, :] != 0
        fixed = (jnp.abs(lanes - i) <= 1) | (lanes < 1)
        left = jnp.where(live & jnp.logical_not(fixed), lanes, n_blocks)
        ids = [0, jnp.maximum(i - 1, 0), i, jnp.minimum(i + 1, n_blocks - 1)]
        last = jnp.int32(-1)
        for _ in range(3):
            last = jnp.min(jnp.where(left > last, left, n_blocks))
            ids.append(jnp.minimum(last, n_blocks - 1))
        for s, j in enumerate(ids):
            copies.append(
                pltpu.make_async_copy(
                    kv_ref.at[pl.ds(pl.multiple_of(j * BLOCK, BLOCK), BLOCK)],
                    near.at[r, pl.ds(s * BLOCK, BLOCK)],
                    sem.at[r, s],
                )
            )
            copies[-1].start()
    slots = len(copies) // rows

    def queries(r):
        return jnp.concatenate(
            [
                q_ref[r * BLOCK : (r + 1) * BLOCK, h * HEAD : (h + 1) * HEAD]
                for h in range(heads)
            ],
            axis=0,
        )

    def put(r, mixed):
        for h in range(heads):
            out_ref[r * BLOCK : (r + 1) * BLOCK, h * HEAD : (h + 1) * HEAD] = mixed[
                h * BLOCK : (h + 1) * BLOCK
            ].astype(jnp.bfloat16)

    for r in range(rows):
        i = blk * rows + r
        for s in range(slots):
            copies[r * slots + s].wait()
        s = score(queries(r), near[r, :, :HEAD])
        parts = [
            jnp.where(i == 1, NEG, s[:, :BLOCK]),
            s[:, BLOCK : 3 * BLOCK],
            jnp.where(i == n_blocks - 1, NEG, s[:, 3 * BLOCK : 4 * BLOCK]),
            s[:, 4 * BLOCK :],
        ]
        s = jnp.concatenate(parts, axis=1)
        top = jnp.max(s, axis=1, keepdims=True)
        p = jnp.exp2(s * SCALE2 - top * SCALE2)
        total = jnp.sum(p, axis=1, keepdims=True)
        mixed = jnp.dot(
            p.astype(jnp.bfloat16), near[r, :, HEAD:], preferred_element_type=jnp.float32
        )
        put(r, mixed / total)

    @pl.when(blk == 0)
    def _():
        keys = chunk * BLOCK
        steps = n_blocks // chunk

        def fetch(step, slot):
            return pltpu.make_async_copy(
                kv_ref.at[pl.ds(pl.multiple_of(step * keys, keys), keys)],
                stream.at[slot],
                stream_sem.at[slot],
            )

        fetch(0, 0).start()
        q = queries(0)
        n = q.shape[0]

        def body(step, state):
            top, total, accum = state
            slot = lax.rem(step, 2)
            fetch(step, slot).wait()

            @pl.when(step + 1 < steps)
            def _():
                fetch(step + 1, 1 - slot).start()

            s = score(q, stream[slot, :, :HEAD])
            new = jnp.maximum(top, jnp.max(s, axis=1, keepdims=True))
            p = jnp.exp2(s * SCALE2 - new * SCALE2)
            factor = jnp.exp2((top - new) * SCALE2)
            total = total * factor + jnp.sum(p, axis=1, keepdims=True)
            accum = accum * factor + jnp.dot(
                p.astype(jnp.bfloat16),
                stream[slot, :, HEAD:],
                preferred_element_type=jnp.float32,
            )
            return new, total, accum

        top, total, accum = lax.fori_loop(
            0,
            steps,
            body,
            (
                jnp.full((n, 1), NEG, jnp.float32),
                jnp.zeros((n, 1), jnp.float32),
                jnp.zeros((n, HEAD), jnp.float32),
            ),
        )
        put(0, accum / total)


def attend(block_mask, q, kv):
    rows = q.shape[0] // BLOCK
    n_blocks = kv.shape[0] // BLOCK
    heads = q.shape[1] // HEAD
    chunk = 8
    vmem = pl.BlockSpec(memory_space=pltpu.VMEM)
    return pl.pallas_call(
        functools.partial(attend_kernel, n_blocks, chunk, heads),
        in_specs=[vmem, vmem, pl.BlockSpec(memory_space=pl.ANY)],
        out_specs=vmem,
        out_shape=jax.ShapeDtypeStruct(q.shape, jnp.bfloat16),
        scratch_shapes=[
            pltpu.VMEM((rows, 7 * BLOCK, 2 * HEAD), jnp.bfloat16),
            pltpu.VMEM((2, chunk * BLOCK, 2 * HEAD), jnp.bfloat16),
            pltpu.SemaphoreType.DMA((rows, 7)),
            pltpu.SemaphoreType.DMA((2,)),
        ],
    )(block_mask, q, kv)


MESH_ID = pl.DeviceIdType.MESH
RING = 4
HALVES = 2


def places():
    g = lax.axis_index("grp")
    col, row = lax.rem(g, RING), g // RING

    def at(dc, flip):
        r = 1 - row if flip else row
        return r * RING + lax.rem(col + dc + RING, RING)

    return at


def greet(peers):
    barrier = pltpu.get_barrier_semaphore()
    for peer in peers:
        pl.semaphore_signal(barrier, inc=1, device_id=peer, device_id_type=MESH_ID)
    pl.semaphore_wait(barrier, len(peers))


def reduce_kernel(
    shard, mixed_ref, w_ref, out_ref,
    terms, far_in, near_in, pair_out, pair_in,
    far_send, far_recv, near_send, near_recv, pair_send, pair_recv,
):
    at = places()
    right, left, pair = at(1, False), at(-1, False), at(0, True)
    side = ({"grp": right}, {"grp": left})
    width = w_ref.shape[1] // HALVES
    FAR, RIGHT, LEFT, OWN = 0, 1, 2, 3
    greet([side[0], side[1], {"grp": pair}])

    def product(slot, dc):
        lhs = jnp.concatenate(
            [
                mixed_ref[pl.ds(pl.multiple_of(at(dc, flip) * shard, shard), shard), :]
                for flip in (True, False)
            ],
            axis=0,
        )
        step = 512
        for half in range(HALVES):
            for c in range(width // step):
                cols = slice(c * step, (c + 1) * step)
                wide = slice(half * width + c * step, half * width + (c + 1) * step)
                t = jnp.dot(lhs, w_ref[:, wide], preferred_element_type=jnp.float32)
                for row in range(2):
                    terms[slot, row, half, :, cols] = t[
                        row * shard : (row + 1) * shard
                    ].astype(jnp.bfloat16)

    def far(row, way):
        return pltpu.make_async_remote_copy(
            terms.at[FAR, row, way], far_in.at[way, row],
            far_send.at[way, row], far_recv.at[way, row],
            device_id=side[way], device_id_type=MESH_ID,
        )

    def near(row, way, half):
        return pltpu.make_async_remote_copy(
            terms.at[RIGHT + way, row, half], near_in.at[way, row, half],
            near_send.at[way, row, half], near_recv.at[way, row, half],
            device_id=side[way], device_id_type=MESH_ID,
        )

    def across(half):
        return pltpu.make_async_remote_copy(
            pair_out.at[half], pair_in.at[half], pair_send.at[half], pair_recv.at[half],
            device_id={"grp": pair}, device_id_type=MESH_ID,
        )

    def carry(row, way):
        far(row, way).wait_recv()
        slot = RIGHT + way
        terms[slot, row, way] = (
            terms[slot, row, way].astype(jnp.float32) + far_in[way, row].astype(jnp.float32)
        ).astype(jnp.bfloat16)
        near(row, way, way).start()

    def gathered(row, half):
        near(row, 0, half).wait_recv()
        near(row, 1, half).wait_recv()
        return (
            terms[OWN, row, half].astype(jnp.float32)
            + near_in[0, row, half].astype(jnp.float32)
            + near_in[1, row, half].astype(jnp.float32)
        )

    product(FAR, 2)
    far(0, 0).start()
    far(0, 1).start()
    product(RIGHT, 1)
    near(0, 0, 1).start()
    product(LEFT, -1)
    near(0, 1, 0).start()
    carry(0, 0)
    carry(0, 1)
    far(1, 0).start()
    far(1, 1).start()
    near(1, 0, 1).start()
    near(1, 1, 0).start()
    product(OWN, 0)
    for half in range(HALVES):
        pair_out[half] = gathered(0, half).astype(jnp.bfloat16)
        across(half).start()
    carry(1, 0)
    carry(1, 1)
    for half in range(HALVES):
        total = gathered(1, half)
        across(half).wait_recv()
        total = total + pair_in[half].astype(jnp.float32)
        out_ref[:, half * width : (half + 1) * width] = total.astype(jnp.bfloat16)
    for row in range(2):
        for way in range(2):
            far(row, way).wait_send()
            for half in range(HALVES):
                near(row, way, half).wait_send()
    for half in range(HALVES):
        across(half).wait_send()


def reduce_out(mixed, w_output, groups):
    rows, width = mixed.shape[0], w_output.shape[1]
    shard, half = rows // groups, width // HALVES
    vmem = pl.BlockSpec(memory_space=pltpu.VMEM)
    dma = pltpu.SemaphoreType.DMA
    piece = (shard, half)
    return pl.pallas_call(
        functools.partial(reduce_kernel, shard),
        in_specs=[vmem, vmem],
        out_specs=vmem,
        out_shape=jax.ShapeDtypeStruct((shard, width), jnp.bfloat16),
        scratch_shapes=[
            pltpu.VMEM((4, 2, HALVES, *piece), jnp.bfloat16),
            pltpu.VMEM((2, 2, *piece), jnp.bfloat16),
            pltpu.VMEM((2, 2, HALVES, *piece), jnp.bfloat16),
            pltpu.VMEM((HALVES, *piece), jnp.bfloat16),
            pltpu.VMEM((HALVES, *piece), jnp.bfloat16),
            dma((2, 2)), dma((2, 2)),
            dma((2, 2, HALVES)), dma((2, 2, HALVES)),
            dma((HALVES,)), dma((HALVES,)),
        ],
        compiler_params=pltpu.CompilerParams(collective_id=1, has_side_effects=True),
    )(mixed, w_output)


def body(tokens, w_query, key_weight, value_weight, w_output, block_mask, positions):
    cosine, sine = rotary_tables(positions)
    piece = lax.all_gather(tokens, "grp", axis=0, tiled=True)
    q, kv = project(piece, w_query, key_weight, value_weight, cosine, sine)
    kv = lax.all_gather(kv, "blk", axis=0, tiled=True)
    mixed = attend(block_mask, q, kv)
    return reduce_out(mixed, w_output, lax.axis_size("grp"))


def solution(mesh):
    return jax.shard_map(
        body,
        mesh=mesh,
        in_specs=(
            P(("blk", "grp"), None),
            P(None, "grp"),
            P(None, "grp"),
            P(None, "grp"),
            P("grp", None),
            P("blk", None),
            P("blk"),
        ),
        out_specs=P(("blk", "grp"), None),
        check_vma=False,
    )
```

```python
import functools

import jax
import jax.numpy as jnp
from jax import lax
from jax.experimental import pallas as pl
from jax.experimental.pallas import tpu as pltpu
from jax.sharding import PartitionSpec as P

HEAD = 128
BLOCK = 128
NEG = -1e30
LOG2E = 1.4426950408889634
SCALE2 = HEAD ** (-0.5) * LOG2E


def rotary_tables(positions):
    half = HEAD // 2
    inverse = jnp.power(
        jnp.float32(500000.0), -(2.0 * jnp.arange(half, dtype=jnp.float32)) / HEAD
    )
    angles = positions.astype(jnp.float32)[:, None] * inverse[None, :]
    cosine, sine = jnp.cos(angles), jnp.sin(angles)
    return (
        jnp.concatenate([cosine, cosine], axis=1),
        jnp.concatenate([-sine, sine], axis=1),
    )


def turn(v, cosine, sine):
    return v * cosine + pltpu.roll(v, HEAD // 2, 1) * sine


def score(q, k):
    return lax.dot_general(q, k, (((1,), (1,)), ((), ())), preferred_element_type=jnp.float32)


def attend_kernel(
    n_blocks, heads, mask_ref, q_ref, kv_ref, out_ref, near, stream, sem, stream_sem
):
    blk = lax.axis_index("blk")
    rows = q_ref.shape[0] // BLOCK
    shard = kv_ref.shape[4]
    pieces = BLOCK // shard
    lanes = lax.broadcasted_iota(jnp.int32, (1, n_blocks), 1)
    for r in range(rows):
        i = blk * rows + r
        live = mask_ref[r : r + 1, :] != 0
        fixed = (jnp.abs(lanes - i) <= 1) | (lanes < 1)
        left = jnp.where(live & jnp.logical_not(fixed), lanes, n_blocks)
        ids = [0, jnp.maximum(i - 1, 0), i, jnp.minimum(i + 1, n_blocks - 1)]
        last = jnp.int32(-1)
        for _ in range(3):
            last = jnp.min(jnp.where(left > last, left, n_blocks))
            ids.append(jnp.minimum(last, n_blocks - 1))
        for s, j in enumerate(ids):
            owner = j // rows
            for h in range(pieces):
                pltpu.make_async_copy(
                    kv_ref.at[
                        lax.rem(owner, 2),
                        owner // 4,
                        lax.rem(j, rows) * pieces + h,
                        lax.rem(owner // 2, 2),
                    ],
                    near.at[r, pl.ds(s * BLOCK + h * shard, shard)],
                    sem.at[r],
                ).start()

    def queries(r):
        return jnp.concatenate(
            [
                q_ref[r * BLOCK : (r + 1) * BLOCK, h * HEAD : (h + 1) * HEAD]
                for h in range(heads)
            ],
            axis=0,
        )

    def put(r, mixed):
        for h in range(heads):
            out_ref[r * BLOCK : (r + 1) * BLOCK, h * HEAD : (h + 1) * HEAD] = mixed[
                h * BLOCK : (h + 1) * BLOCK
            ].astype(jnp.bfloat16)

    for r in range(rows):
        i = blk * rows + r
        pltpu.make_async_copy(near.at[r], near.at[r], sem.at[r]).wait()
        s = score(queries(r), near[r, :, :HEAD])
        parts = [
            jnp.where(i == 1, NEG, s[:, :BLOCK]),
            s[:, BLOCK : 3 * BLOCK],
            jnp.where(i == n_blocks - 1, NEG, s[:, 3 * BLOCK : 4 * BLOCK]),
            s[:, 4 * BLOCK :],
        ]
        s = jnp.concatenate(parts, axis=1)
        top = jnp.max(s, axis=1, keepdims=True)
        p = jnp.exp2(s * SCALE2 - top * SCALE2)
        total = jnp.sum(p, axis=1, keepdims=True)
        mixed = jnp.dot(
            p.astype(jnp.bfloat16), near[r, :, HEAD:], preferred_element_type=jnp.float32
        )
        put(r, mixed / total)

    @pl.when(blk == 0)
    def _():
        steps = kv_ref.shape[0] * kv_ref.shape[1]

        def fetch(step, slot):
            return pltpu.make_async_copy(
                kv_ref.at[step // kv_ref.shape[1], lax.rem(step, kv_ref.shape[1])],
                stream.at[slot],
                stream_sem.at[slot],
            )

        fetch(0, 0).start()
        q = queries(0)
        n = q.shape[0]

        def body(step, state):
            top, total, accum = state
            slot = lax.rem(step, 2)
            fetch(step, slot).wait()

            @pl.when(step + 1 < steps)
            def _():
                fetch(step + 1, 1 - slot).start()

            both = stream[slot].reshape(-1, 2 * HEAD)
            s = score(q, both[:, :HEAD])
            new = jnp.maximum(top, jnp.max(s, axis=1, keepdims=True))
            p = jnp.exp2(s * SCALE2 - new * SCALE2)
            factor = jnp.exp2((top - new) * SCALE2)
            total = total * factor + jnp.sum(p, axis=1, keepdims=True)
            accum = accum * factor + jnp.dot(
                p.astype(jnp.bfloat16),
                both[:, HEAD:],
                preferred_element_type=jnp.float32,
            )
            return new, total, accum

        top, total, accum = lax.fori_loop(
            0,
            steps,
            body,
            (
                jnp.full((n, 1), NEG, jnp.float32),
                jnp.zeros((n, 1), jnp.float32),
                jnp.zeros((n, HEAD), jnp.float32),
            ),
        )
        put(0, accum / total)


def attend(block_mask, q, kv):
    rows = q.shape[0] // BLOCK
    n_blocks = block_mask.shape[1]
    heads = q.shape[1] // HEAD
    vmem = pl.BlockSpec(memory_space=pltpu.VMEM)
    return pl.pallas_call(
        functools.partial(attend_kernel, n_blocks, heads),
        in_specs=[vmem, vmem, pl.BlockSpec(memory_space=pl.ANY)],
        out_specs=vmem,
        out_shape=jax.ShapeDtypeStruct(q.shape, jnp.bfloat16),
        scratch_shapes=[
            pltpu.VMEM((rows, 7 * BLOCK, 2 * HEAD), jnp.bfloat16),
            pltpu.VMEM((2, *kv.shape[2:]), jnp.bfloat16),
            pltpu.SemaphoreType.DMA((rows,)),
            pltpu.SemaphoreType.DMA((2,)),
        ],
    )(block_mask, q, kv)


MESH_ID = pl.DeviceIdType.MESH
RING = 4
HALVES = 2


def places():
    g = lax.axis_index("grp")
    col, row = lax.rem(g, RING), g // RING

    def at(dc, flip):
        r = 1 - row if flip else row
        return r * RING + lax.rem(col + dc + RING, RING)

    return at


def greet(peers):
    barrier = pltpu.get_barrier_semaphore()
    for peer in peers:
        pl.semaphore_signal(barrier, inc=1, device_id=peer, device_id_type=MESH_ID)
    pl.semaphore_wait(barrier, len(peers))


def reduce_kernel(
    shard, mixed_ref, w_ref, out_ref,
    terms, far_in, near_in, pair_out, pair_in,
    far_send, far_recv, near_send, near_recv, pair_send, pair_recv,
):
    at = places()
    right, left, pair = at(1, False), at(-1, False), at(0, True)
    side = ({"grp": right}, {"grp": left})
    width = w_ref.shape[1] // HALVES
    FAR, RIGHT, LEFT, OWN = 0, 1, 2, 3
    greet([side[0], side[1], {"grp": pair}])

    def product(slot, dc):
        lhs = jnp.concatenate(
            [
                mixed_ref[pl.ds(pl.multiple_of(at(dc, flip) * shard, shard), shard), :]
                for flip in (True, False)
            ],
            axis=0,
        )
        step = 512
        for half in range(HALVES):
            for c in range(width // step):
                cols = slice(c * step, (c + 1) * step)
                wide = slice(half * width + c * step, half * width + (c + 1) * step)
                t = jnp.dot(lhs, w_ref[:, wide], preferred_element_type=jnp.float32)
                for row in range(2):
                    terms[slot, row, half, :, cols] = t[
                        row * shard : (row + 1) * shard
                    ].astype(jnp.bfloat16)

    def far(row, way):
        return pltpu.make_async_remote_copy(
            terms.at[FAR, row, way], far_in.at[way, row],
            far_send.at[way, row], far_recv.at[way, row],
            device_id=side[way], device_id_type=MESH_ID,
        )

    def near(row, way, half):
        return pltpu.make_async_remote_copy(
            terms.at[RIGHT + way, row, half], near_in.at[way, row, half],
            near_send.at[way, row, half], near_recv.at[way, row, half],
            device_id=side[way], device_id_type=MESH_ID,
        )

    def across(half):
        return pltpu.make_async_remote_copy(
            pair_out.at[half], pair_in.at[half], pair_send.at[half], pair_recv.at[half],
            device_id={"grp": pair}, device_id_type=MESH_ID,
        )

    def carry(row, way):
        far(row, way).wait_recv()
        slot = RIGHT + way
        terms[slot, row, way] = (
            terms[slot, row, way].astype(jnp.float32) + far_in[way, row].astype(jnp.float32)
        ).astype(jnp.bfloat16)
        near(row, way, way).start()

    def gathered(row, half):
        near(row, 0, half).wait_recv()
        near(row, 1, half).wait_recv()
        return (
            terms[OWN, row, half].astype(jnp.float32)
            + near_in[0, row, half].astype(jnp.float32)
            + near_in[1, row, half].astype(jnp.float32)
        )

    product(FAR, 2)
    far(0, 0).start()
    far(0, 1).start()
    product(RIGHT, 1)
    near(0, 0, 1).start()
    product(LEFT, -1)
    near(0, 1, 0).start()
    carry(0, 0)
    carry(0, 1)
    far(1, 0).start()
    far(1, 1).start()
    near(1, 0, 1).start()
    near(1, 1, 0).start()
    product(OWN, 0)
    for half in range(HALVES):
        pair_out[half] = gathered(0, half).astype(jnp.bfloat16)
        across(half).start()
    carry(1, 0)
    carry(1, 1)
    for half in range(HALVES):
        total = gathered(1, half)
        across(half).wait_recv()
        total = total + pair_in[half].astype(jnp.float32)
        out_ref[:, half * width : (half + 1) * width] = total.astype(jnp.bfloat16)
    for row in range(2):
        for way in range(2):
            far(row, way).wait_send()
            for half in range(HALVES):
                near(row, way, half).wait_send()
    for half in range(HALVES):
        across(half).wait_send()


def reduce_out(mixed, w_output, groups):
    rows, width = mixed.shape[0], w_output.shape[1]
    shard, half = rows // groups, width // HALVES
    vmem = pl.BlockSpec(memory_space=pltpu.VMEM)
    dma = pltpu.SemaphoreType.DMA
    piece = (shard, half)
    return pl.pallas_call(
        functools.partial(reduce_kernel, shard),
        in_specs=[vmem, vmem],
        out_specs=vmem,
        out_shape=jax.ShapeDtypeStruct((shard, width), jnp.bfloat16),
        scratch_shapes=[
            pltpu.VMEM((4, 2, HALVES, *piece), jnp.bfloat16),
            pltpu.VMEM((2, 2, *piece), jnp.bfloat16),
            pltpu.VMEM((2, 2, HALVES, *piece), jnp.bfloat16),
            pltpu.VMEM((HALVES, *piece), jnp.bfloat16),
            pltpu.VMEM((HALVES, *piece), jnp.bfloat16),
            dma((2, 2)), dma((2, 2)),
            dma((2, 2, HALVES)), dma((2, 2, HALVES)),
            dma((HALVES,)), dma((HALVES,)),
        ],
        compiler_params=pltpu.CompilerParams(collective_id=1, has_side_effects=True),
    )(mixed, w_output)


Z_RING = 8


def gather_kernel(
    tokens_ref, wq_ref, wk_ref, wv_ref, cos_ref, sin_ref, q_ref, kv_ref,
    tok, wq, wkv, mine,
    load_sem, own_send, own_recv, far_send, far_recv,
    mine_sem, y_send, y_recv, z_send, z_recv, core_send, core_recv,
):
    at = places()
    side = ({"grp": at(1, False)}, {"grp": at(-1, False)})
    pair = {"grp": at(0, True)}
    blk = lax.axis_index("blk")
    core, near_y, depth = lax.rem(blk, 2), lax.rem(blk // 2, 2), blk // 4
    shard, half = tokens_ref.shape[0], tokens_ref.shape[0] // 2

    def deep(step):
        return lax.rem(depth + step + Z_RING, Z_RING)

    z_side = tuple({"blk": (deep(d) * 2 + near_y) * 2 + core} for d in (1, -1))
    y_side = {"blk": (depth * 2 + 1 - near_y) * 2 + core}
    core_side = {"blk": (depth * 2 + near_y) * 2 + 1 - core}

    loads = [
        pltpu.make_async_copy(tokens_ref, tok.at[0, 0], load_sem.at[0]),
        pltpu.make_async_copy(wk_ref, wkv.at[:, pl.ds(0, HEAD)], load_sem.at[1]),
        pltpu.make_async_copy(wv_ref, wkv.at[:, pl.ds(HEAD, HEAD)], load_sem.at[2]),
        pltpu.make_async_copy(wq_ref, wq, load_sem.at[3]),
    ]
    for load in loads:
        load.start()
    greet([*side, pair, *z_side, y_side, core_side])

    def rows(row, place, h):
        return tok.at[row, place, pl.ds(h * half, half)]

    def hand(row, way, h):
        return pltpu.make_async_remote_copy(
            rows(row, 0, h), rows(row, 1 + way, h),
            own_send.at[row, way, h], own_recv.at[row, way, h],
            device_id=side[way], device_id_type=MESH_ID,
        )

    def cross(h):
        return pltpu.make_async_remote_copy(
            rows(0, 0, h), rows(1, 0, h), own_send.at[0, 2, h], own_recv.at[0, 2, h],
            device_id=pair, device_id_type=MESH_ID,
        )

    def further(row, way):
        return pltpu.make_async_remote_copy(
            rows(row, 1 + way, way), rows(row, 3, way),
            far_send.at[row, way], far_recv.at[row, way],
            device_id=side[way], device_id_type=MESH_ID,
        )

    def hand_on(row):
        for h in range(2):
            hand(row, 0, h).start()
            hand(row, 1, 1 - h).start()

    def pass_on(row):
        for way in range(2):
            hand(row, way, way).wait_recv()
            further(row, way).start()

    order = ((0, 0, 0), (0, 1, -1), (0, 2, 1), (0, 3, 2), (1, 0, 0), (1, 1, -1), (1, 2, 1), (1, 3, 2))

    def spot(u):
        row, _, dc = order[u]
        return at(dc, row == 1)

    def tables(u):
        here = pl.ds(pl.multiple_of(spot(u) * shard, shard), shard)
        return cos_ref[here, :], sin_ref[here, :]

    def keep(u):
        return pltpu.make_async_copy(
            mine.at[u], kv_ref.at[core, depth, spot(u), near_y], mine_sem.at[u]
        )

    def y_copy(u):
        return pltpu.make_async_remote_copy(
            mine.at[u], kv_ref.at[core, depth, spot(u), near_y],
            y_send.at[u], y_recv.at[u],
            device_id=y_side, device_id_type=MESH_ID,
        )

    def z_copy(u, way, hop):
        origin = deep(-hop if way == 0 else hop)
        ref = kv_ref.at[core, origin, spot(u)]
        if hop == 3:
            ref = kv_ref.at[core, origin, spot(u), way]
        return pltpu.make_async_remote_copy(
            ref, ref, z_send.at[way, hop, u], z_recv.at[way, hop, u],
            device_id=z_side[way], device_id_type=MESH_ID,
        )

    def z_arrival(u, way, hop):
        origin = deep(-hop - 1 if way == 0 else hop + 1)
        ref = kv_ref.at[core, origin, spot(u)]
        if hop == 3:
            ref = kv_ref.at[core, origin, spot(u), way]
        return pltpu.make_async_remote_copy(
            ref, ref, z_send.at[way, hop, u], z_recv.at[way, hop, u],
            device_id=z_side[way], device_id_type=MESH_ID,
        )

    def core_copy(u, origin):
        ref = kv_ref.at[core, origin, spot(u)]
        return pltpu.make_async_remote_copy(
            ref, ref, core_send, core_recv, device_id=core_side, device_id_type=MESH_ID
        )

    def keys(u):
        row, place, _ = order[u]
        y = jnp.dot(tok[row, place], wkv[...], preferred_element_type=jnp.float32)
        cosine, sine = tables(u)
        mine[u, :, :HEAD] = turn(y[:, :HEAD], cosine, sine).astype(jnp.bfloat16)
        mine[u, :, HEAD:] = y[:, HEAD:].astype(jnp.bfloat16)
        keep(u).start()
        y_copy(u).start()

    def ring(u, stage):
        if stage == 0:
            keep(u).wait()
            y_copy(u).wait_recv()
            z_copy(u, 0, 0).start()
            z_copy(u, 1, 0).start()
            core_copy(u, depth).start()
            return
        for way in range(2):
            z_arrival(u, way, stage - 1).wait_recv()
            if stage < 4:
                z_copy(u, way, stage).start()
                core_copy(u, deep(-stage if way == 0 else stage)).start()
        if stage == 4:
            core_copy(u, deep(4)).start()

    def queries(row, part):
        wide = 2 * HEAD
        x = tok[row].reshape(4 * shard, tok.shape[-1])
        cols = slice(part * wide, (part + 1) * wide)
        y = jnp.dot(x, wq[:, cols], preferred_element_type=jnp.float32)
        for n in range(4):
            u = next(i for i, o in enumerate(order) if o[:2] == (row, n))
            cosine, sine = tables(u)
            here = pl.ds(pl.multiple_of(spot(u) * shard, shard), shard)
            for h in range(2):
                v = y[n * shard : (n + 1) * shard, h * HEAD : (h + 1) * HEAD]
                q_ref[here, part * wide + h * HEAD : part * wide + (h + 1) * HEAD] = turn(
                    v, cosine, sine
                ).astype(jnp.bfloat16)

    loads[0].wait()
    hand_on(0)
    for h in range(2):
        cross(h).start()
    loads[1].wait()
    loads[2].wait()
    keys(0)
    ring(0, 0)
    pass_on(0)
    ring(0, 1)
    ring(0, 2)
    hand(0, 0, 1).wait_recv()
    keys(1)
    hand(0, 1, 0).wait_recv()
    keys(2)
    ring(0, 3)
    ring(1, 0)
    ring(2, 0)
    for h in range(2):
        cross(h).wait_recv()
    hand_on(1)
    ring(0, 4)
    ring(1, 1)
    ring(2, 1)
    further(0, 0).wait_recv()
    further(0, 1).wait_recv()
    keys(3)
    keys(4)
    ring(1, 2)
    ring(2, 2)
    ring(3, 0)
    ring(4, 0)
    loads[3].wait()
    queries(0, 0)
    ring(1, 3)
    ring(2, 3)
    ring(3, 1)
    ring(4, 1)
    queries(0, 1)
    pass_on(1)
    ring(1, 4)
    ring(2, 4)
    ring(3, 2)
    ring(4, 2)
    hand(1, 0, 1).wait_recv()
    keys(5)
    hand(1, 1, 0).wait_recv()
    keys(6)
    ring(3, 3)
    ring(4, 3)
    ring(5, 0)
    ring(6, 0)
    further(1, 0).wait_recv()
    further(1, 1).wait_recv()
    keys(7)
    ring(3, 4)
    ring(4, 4)
    ring(5, 1)
    ring(6, 1)
    ring(7, 0)
    queries(1, 0)
    ring(5, 2)
    ring(6, 2)
    ring(7, 1)
    queries(1, 1)
    for stage in (3, 4):
        ring(5, stage)
        ring(6, stage)
        ring(7, stage - 1)
    ring(7, 4)

    for h in range(2):
        cross(h).wait_send()
        for row in range(2):
            for way in range(2):
                hand(row, way, h).wait_send()
    for row in range(2):
        for way in range(2):
            further(row, way).wait_send()
    for u in range(len(order)):
        y_copy(u).wait_send()
        for way in range(2):
            for hop in range(4):
                z_copy(u, way, hop).wait_send()
    done = kv_ref.at[core]
    pltpu.make_async_copy(done, done, core_send).wait()
    done = kv_ref.at[1 - core]
    pltpu.make_async_copy(done, done, core_recv).wait()


def gather(tokens, wq, wk, wv, cosine, sine, groups):
    shard, width = tokens.shape
    units = groups
    hbm, vmem = pl.BlockSpec(memory_space=pl.ANY), pl.BlockSpec(memory_space=pltpu.VMEM)
    dma = pltpu.SemaphoreType.DMA
    return pl.pallas_call(
        gather_kernel,
        in_specs=[hbm, hbm, hbm, hbm, vmem, vmem],
        out_specs=[vmem, hbm],
        out_shape=[
            jax.ShapeDtypeStruct((shard * groups, wq.shape[1]), jnp.bfloat16),
            jax.ShapeDtypeStruct((2, Z_RING, groups, 2, shard, 2 * HEAD), jnp.bfloat16),
        ],
        scratch_shapes=[
            pltpu.VMEM((2, RING, shard, width), jnp.bfloat16),
            pltpu.VMEM(wq.shape, jnp.bfloat16),
            pltpu.VMEM((width, 2 * HEAD), jnp.bfloat16),
            pltpu.VMEM((units, shard, 2 * HEAD), jnp.bfloat16),
            dma((4,)),
            dma((2, 3, 2)), dma((2, 3, 2)), dma((2, 2)), dma((2, 2)),
            dma((units,)), dma((units,)), dma((units,)),
            dma((2, 4, units)), dma((2, 4, units)),
            dma, dma,
        ],
        compiler_params=pltpu.CompilerParams(collective_id=0, has_side_effects=True),
    )(tokens, wq, wk, wv, cosine, sine)


def body(tokens, w_query, key_weight, value_weight, w_output, block_mask, positions):
    cosine, sine = rotary_tables(positions)
    groups = lax.axis_size("grp")
    q, kv = gather(tokens, w_query, key_weight, value_weight, cosine, sine, groups)
    mixed = attend(block_mask, q, kv)
    return reduce_out(mixed, w_output, groups)


def solution(mesh):
    return jax.shard_map(
        body,
        mesh=mesh,
        in_specs=(
            P(("blk", "grp"), None),
            P(None, "grp"),
            P(None, "grp"),
            P(None, "grp"),
            P("grp", None),
            P("blk", None),
            P("blk"),
        ),
        out_specs=P(("blk", "grp"), None),
        check_vma=False,
    )
```

```python
import functools

import jax
import jax.numpy as jnp
from jax import lax
from jax.experimental import pallas as pl
from jax.experimental.pallas import tpu as pltpu
from jax.sharding import PartitionSpec as P

HEAD = 128
BLOCK = 128
NEG = -1e30
LOG2E = 1.4426950408889634
SCALE2 = HEAD ** (-0.5) * LOG2E


def rotary_tables(positions):
    half = HEAD // 2
    inverse = jnp.power(
        jnp.float32(500000.0), -(2.0 * jnp.arange(half, dtype=jnp.float32)) / HEAD
    )
    angles = positions.astype(jnp.float32)[:, None] * inverse[None, :]
    cosine, sine = jnp.cos(angles), jnp.sin(angles)
    return (
        jnp.concatenate([cosine, cosine], axis=1),
        jnp.concatenate([-sine, sine], axis=1),
    )


def turn(v, cosine, sine):
    return v * cosine + pltpu.roll(v, HEAD // 2, 1) * sine


def score(q, k):
    return lax.dot_general(q, k, (((1,), (1,)), ((), ())), preferred_element_type=jnp.float32)


def attend_kernel(
    n_blocks, heads, mask_ref, q_ref, kv_ref, out_ref, near, stream, sem, stream_sem
):
    blk = lax.axis_index("blk")
    rows = q_ref.shape[0] // BLOCK
    shard = kv_ref.shape[4]
    pieces = BLOCK // shard
    lanes = lax.broadcasted_iota(jnp.int32, (1, n_blocks), 1)
    for r in range(rows):
        i = blk * rows + r
        live = mask_ref[r : r + 1, :] != 0
        fixed = (jnp.abs(lanes - i) <= 1) | (lanes < 1)
        left = jnp.where(live & jnp.logical_not(fixed), lanes, n_blocks)
        ids = [0, jnp.maximum(i - 1, 0), i, jnp.minimum(i + 1, n_blocks - 1)]
        last = jnp.int32(-1)
        for _ in range(3):
            last = jnp.min(jnp.where(left > last, left, n_blocks))
            ids.append(jnp.minimum(last, n_blocks - 1))
        for s, j in enumerate(ids):
            owner = j // rows
            for h in range(pieces):
                pltpu.make_async_copy(
                    kv_ref.at[
                        lax.rem(owner, 2),
                        owner // 4,
                        lax.rem(j, rows) * pieces + h,
                        lax.rem(owner // 2, 2),
                    ],
                    near.at[r, pl.ds(s * BLOCK + h * shard, shard)],
                    sem.at[r],
                ).start()

    def queries(r):
        return jnp.concatenate(
            [
                q_ref[r * BLOCK : (r + 1) * BLOCK, h * HEAD : (h + 1) * HEAD]
                for h in range(heads)
            ],
            axis=0,
        )

    def put(r, mixed):
        for h in range(heads):
            out_ref[r * BLOCK : (r + 1) * BLOCK, h * HEAD : (h + 1) * HEAD] = mixed[
                h * BLOCK : (h + 1) * BLOCK
            ].astype(jnp.bfloat16)

    for r in range(rows):
        i = blk * rows + r
        pltpu.make_async_copy(near.at[r], near.at[r], sem.at[r]).wait()
        s = score(queries(r), near[r, :, :HEAD])
        parts = [
            jnp.where(i == 1, NEG, s[:, :BLOCK]),
            s[:, BLOCK : 3 * BLOCK],
            jnp.where(i == n_blocks - 1, NEG, s[:, 3 * BLOCK : 4 * BLOCK]),
            s[:, 4 * BLOCK :],
        ]
        s = jnp.concatenate(parts, axis=1)
        top = jnp.max(s, axis=1, keepdims=True)
        p = jnp.exp2(s * SCALE2 - top * SCALE2)
        total = jnp.sum(p, axis=1, keepdims=True)
        mixed = jnp.dot(
            p.astype(jnp.bfloat16), near[r, :, HEAD:], preferred_element_type=jnp.float32
        )
        put(r, mixed / total)

    @pl.when(blk == 0)
    def _():
        steps = kv_ref.shape[0] * kv_ref.shape[1]

        def fetch(step, slot):
            return pltpu.make_async_copy(
                kv_ref.at[step // kv_ref.shape[1], lax.rem(step, kv_ref.shape[1])],
                stream.at[slot],
                stream_sem.at[slot],
            )

        fetch(0, 0).start()
        q = queries(0)
        n = q.shape[0]

        def body(step, state):
            top, total, accum = state
            slot = lax.rem(step, 2)
            fetch(step, slot).wait()

            @pl.when(step + 1 < steps)
            def _():
                fetch(step + 1, 1 - slot).start()

            both = stream[slot].reshape(-1, 2 * HEAD)
            s = score(q, both[:, :HEAD])
            new = jnp.maximum(top, jnp.max(s, axis=1, keepdims=True))
            p = jnp.exp2(s * SCALE2 - new * SCALE2)
            factor = jnp.exp2((top - new) * SCALE2)
            total = total * factor + jnp.sum(p, axis=1, keepdims=True)
            accum = accum * factor + jnp.dot(
                p.astype(jnp.bfloat16),
                both[:, HEAD:],
                preferred_element_type=jnp.float32,
            )
            return new, total, accum

        top, total, accum = lax.fori_loop(
            0,
            steps,
            body,
            (
                jnp.full((n, 1), NEG, jnp.float32),
                jnp.zeros((n, 1), jnp.float32),
                jnp.zeros((n, HEAD), jnp.float32),
            ),
        )
        put(0, accum / total)


def attend(block_mask, q, kv):
    rows = q.shape[0] // BLOCK
    n_blocks = block_mask.shape[1]
    heads = q.shape[1] // HEAD
    vmem = pl.BlockSpec(memory_space=pltpu.VMEM)
    return pl.pallas_call(
        functools.partial(attend_kernel, n_blocks, heads),
        in_specs=[vmem, vmem, pl.BlockSpec(memory_space=pl.ANY)],
        out_specs=vmem,
        out_shape=jax.ShapeDtypeStruct(q.shape, jnp.bfloat16),
        scratch_shapes=[
            pltpu.VMEM((rows, 7 * BLOCK, 2 * HEAD), jnp.bfloat16),
            pltpu.VMEM((2, *kv.shape[2:]), jnp.bfloat16),
            pltpu.SemaphoreType.DMA((rows,)),
            pltpu.SemaphoreType.DMA((2,)),
        ],
    )(block_mask, q, kv)


MESH_ID = pl.DeviceIdType.MESH
RING = 4
HALVES = 2


def places():
    g = lax.axis_index("grp")
    col, row = lax.rem(g, RING), g // RING

    def at(dc, flip):
        r = 1 - row if flip else row
        return r * RING + lax.rem(col + dc + RING, RING)

    return at


def greet(peers):
    barrier = pltpu.get_barrier_semaphore()
    for peer in peers:
        pl.semaphore_signal(barrier, inc=1, device_id=peer, device_id_type=MESH_ID)
    pl.semaphore_wait(barrier, len(peers))


def reduce_kernel(
    shard, mixed_ref, w_ref, out_ref,
    terms, far_in, near_in, pair_out, pair_in,
    far_send, far_recv, near_send, near_recv, pair_send, pair_recv,
):
    at = places()
    right, left, pair = at(1, False), at(-1, False), at(0, True)
    side = ({"grp": right}, {"grp": left})
    width = w_ref.shape[1] // HALVES
    FAR, RIGHT, LEFT, OWN = 0, 1, 2, 3
    greet([side[0], side[1], {"grp": pair}])

    def product(slot, dc):
        lhs = jnp.concatenate(
            [
                mixed_ref[pl.ds(pl.multiple_of(at(dc, flip) * shard, shard), shard), :]
                for flip in (True, False)
            ],
            axis=0,
        )
        step = 512
        for half in range(HALVES):
            for c in range(width // step):
                cols = slice(c * step, (c + 1) * step)
                wide = slice(half * width + c * step, half * width + (c + 1) * step)
                t = jnp.dot(lhs, w_ref[:, wide], preferred_element_type=jnp.float32)
                for row in range(2):
                    terms[slot, row, half, :, cols] = t[
                        row * shard : (row + 1) * shard
                    ].astype(jnp.bfloat16)

    def far(row, way):
        return pltpu.make_async_remote_copy(
            terms.at[FAR, row, way], far_in.at[way, row],
            far_send.at[way, row], far_recv.at[way, row],
            device_id=side[way], device_id_type=MESH_ID,
        )

    def near(row, way, half):
        return pltpu.make_async_remote_copy(
            terms.at[RIGHT + way, row, half], near_in.at[way, row, half],
            near_send.at[way, row, half], near_recv.at[way, row, half],
            device_id=side[way], device_id_type=MESH_ID,
        )

    def across(half):
        return pltpu.make_async_remote_copy(
            pair_out.at[half], pair_in.at[half], pair_send.at[half], pair_recv.at[half],
            device_id={"grp": pair}, device_id_type=MESH_ID,
        )

    def carry(row, way):
        far(row, way).wait_recv()
        slot = RIGHT + way
        terms[slot, row, way] = (
            terms[slot, row, way].astype(jnp.float32) + far_in[way, row].astype(jnp.float32)
        ).astype(jnp.bfloat16)
        near(row, way, way).start()

    def gathered(row, half):
        near(row, 0, half).wait_recv()
        near(row, 1, half).wait_recv()
        return (
            terms[OWN, row, half].astype(jnp.float32)
            + near_in[0, row, half].astype(jnp.float32)
            + near_in[1, row, half].astype(jnp.float32)
        )

    product(FAR, 2)
    far(0, 0).start()
    far(0, 1).start()
    product(RIGHT, 1)
    near(0, 0, 1).start()
    product(LEFT, -1)
    near(0, 1, 0).start()
    carry(0, 0)
    carry(0, 1)
    far(1, 0).start()
    far(1, 1).start()
    near(1, 0, 1).start()
    near(1, 1, 0).start()
    product(OWN, 0)
    for half in range(HALVES):
        pair_out[half] = gathered(0, half).astype(jnp.bfloat16)
        across(half).start()
    carry(1, 0)
    carry(1, 1)
    for half in range(HALVES):
        total = gathered(1, half)
        across(half).wait_recv()
        total = total + pair_in[half].astype(jnp.float32)
        out_ref[:, half * width : (half + 1) * width] = total.astype(jnp.bfloat16)
    for row in range(2):
        for way in range(2):
            far(row, way).wait_send()
            for half in range(HALVES):
                near(row, way, half).wait_send()
    for half in range(HALVES):
        across(half).wait_send()


def reduce_out(mixed, w_output, groups):
    rows, width = mixed.shape[0], w_output.shape[1]
    shard, half = rows // groups, width // HALVES
    vmem = pl.BlockSpec(memory_space=pltpu.VMEM)
    dma = pltpu.SemaphoreType.DMA
    piece = (shard, half)
    return pl.pallas_call(
        functools.partial(reduce_kernel, shard),
        in_specs=[vmem, vmem],
        out_specs=vmem,
        out_shape=jax.ShapeDtypeStruct((shard, width), jnp.bfloat16),
        scratch_shapes=[
            pltpu.VMEM((4, 2, HALVES, *piece), jnp.bfloat16),
            pltpu.VMEM((2, 2, *piece), jnp.bfloat16),
            pltpu.VMEM((2, 2, HALVES, *piece), jnp.bfloat16),
            pltpu.VMEM((HALVES, *piece), jnp.bfloat16),
            pltpu.VMEM((HALVES, *piece), jnp.bfloat16),
            dma((2, 2)), dma((2, 2)),
            dma((2, 2, HALVES)), dma((2, 2, HALVES)),
            dma((HALVES,)), dma((HALVES,)),
        ],
        compiler_params=pltpu.CompilerParams(collective_id=1, has_side_effects=True),
    )(mixed, w_output)


Z_RING = 8
RELAY = False
SPLIT = (0, 3, 4, 5, 7)
ORDER = (
    (2, 0, 0, 0), (4, 0, 0, 0), (5, 0, 0, 0), (4, 0, 1, 0), (4, 0, 1, 1), (0, 0, 0, 0),
    (0, 0, 1, 0), (1, 0, 0, 0), (4, 0, 2, 0), (4, 0, 2, 1), (5, 0, 1, 0), (5, 0, 1, 1),
    (4, 0, 3, 0), (2, 1, 0, 0), (1, 1, 0, 0), (2, 2, 0, 0), (2, 4, 0, 0), (4, 4, 0, 0),
    (2, 3, 0, 0), (4, 3, 0, 0), (4, 2, 0, 0), (4, 1, 0, 0), (4, 0, 3, 1), (4, 0, 4, 0),
    (5, 0, 2, 0), (5, 0, 2, 1), (5, 0, 3, 0), (4, 4, 1, 0), (4, 4, 1, 1), (5, 4, 0, 0),
    (3, 0, 0, 0), (0, 1, 0, 0), (4, 3, 1, 0), (4, 3, 1, 1), (5, 0, 3, 1), (5, 3, 0, 0),
    (3, 0, 1, 0), (4, 2, 1, 0), (4, 2, 1, 1), (4, 1, 1, 0), (4, 1, 1, 1), (4, 4, 2, 0),
    (4, 4, 2, 1), (5, 0, 4, 0), (4, 3, 2, 0), (4, 3, 2, 1), (5, 3, 1, 0), (0, 1, 1, 0),
    (2, 5, 0, 0), (2, 6, 0, 0), (4, 5, 0, 0), (4, 2, 2, 0), (4, 2, 2, 1), (4, 1, 2, 0),
    (4, 4, 3, 0), (4, 4, 3, 1), (4, 1, 2, 1), (4, 3, 3, 0), (4, 3, 3, 1), (5, 3, 1, 1),
    (5, 3, 2, 0), (5, 3, 2, 1), (5, 4, 1, 0), (5, 4, 1, 1), (5, 4, 2, 0), (5, 4, 2, 1),
    (5, 5, 0, 0), (4, 6, 0, 0), (4, 5, 1, 0), (4, 5, 1, 1), (5, 4, 3, 0), (2, 7, 0, 0),
    (4, 7, 0, 0), (4, 2, 3, 0), (4, 2, 3, 1), (4, 1, 3, 0), (4, 4, 4, 0), (4, 3, 4, 1),
    (4, 1, 3, 1), (5, 3, 3, 0), (5, 3, 3, 1), (5, 4, 3, 1), (5, 5, 1, 0), (3, 1, 0, 0),
    (4, 6, 1, 0), (4, 7, 1, 0), (4, 7, 1, 1), (4, 6, 1, 1), (4, 5, 2, 0), (4, 5, 2, 1),
    (4, 2, 4, 0), (4, 2, 4, 1), (4, 1, 4, 0), (4, 1, 4, 1), (5, 3, 4, 1), (5, 4, 4, 0),
    (5, 5, 1, 1), (5, 7, 0, 0), (3, 1, 1, 0), (4, 7, 2, 1), (4, 6, 2, 0), (5, 7, 1, 0),
    (5, 7, 1, 1), (4, 7, 2, 0), (5, 5, 2, 0), (4, 6, 2, 1), (4, 5, 3, 0), (5, 5, 2, 1),
    (4, 5, 3, 1), (4, 7, 3, 1), (5, 7, 2, 1), (4, 6, 3, 0), (5, 7, 2, 0), (4, 7, 3, 0),
    (5, 5, 3, 0), (4, 6, 3, 1), (5, 5, 3, 1), (4, 5, 4, 1), (4, 7, 4, 1), (5, 7, 3, 1),
    (4, 6, 4, 0), (5, 7, 3, 0), (4, 6, 4, 1), (5, 5, 4, 1), (5, 7, 4, 1),
)


def gather_kernel(
    tokens_ref, wq_ref, wk_ref, wv_ref, cos_ref, sin_ref, q_ref, kv_ref,
    tok, wq, wkv, mine,
    load_sem, own_send, own_recv, far_send, far_recv,
    mine_sem, y_send, y_recv, z_send, z_recv, fwd_send, fwd_recv, core_send, core_recv,
):
    at = places()
    side = ({"grp": at(1, False)}, {"grp": at(-1, False)})
    pair = {"grp": at(0, True)}
    blk = lax.axis_index("blk")
    core, near_y, depth = lax.rem(blk, 2), lax.rem(blk // 2, 2), blk // 4
    shard, half = tokens_ref.shape[0], tokens_ref.shape[0] // 2

    def deep(step):
        return lax.rem(depth + step + Z_RING, Z_RING)

    z_side = tuple({"blk": (deep(d) * 2 + near_y) * 2 + core} for d in (1, -1))
    y_side = {"blk": (depth * 2 + 1 - near_y) * 2 + core}
    core_side = {"blk": (depth * 2 + near_y) * 2 + 1 - core}

    loads = [
        pltpu.make_async_copy(tokens_ref, tok.at[0, 0], load_sem.at[0]),
        pltpu.make_async_copy(wk_ref, wkv.at[:, pl.ds(0, HEAD)], load_sem.at[1]),
        pltpu.make_async_copy(wv_ref, wkv.at[:, pl.ds(HEAD, HEAD)], load_sem.at[2]),
        pltpu.make_async_copy(wq_ref, wq, load_sem.at[3]),
    ]
    for load in loads:
        load.start()
    greet([*side, pair, *z_side, y_side, core_side])

    def rows(row, place, h):
        return tok.at[row, place, pl.ds(h * half, half)]

    def hand(row, way, h):
        return pltpu.make_async_remote_copy(
            rows(row, 0, h), rows(row, 1 + way, h),
            own_send.at[row, way, h], own_recv.at[row, way, h],
            device_id=side[way], device_id_type=MESH_ID,
        )

    def cross(h):
        return pltpu.make_async_remote_copy(
            rows(0, 0, h), rows(1, 0, h), own_send.at[0, 2, h], own_recv.at[0, 2, h],
            device_id=pair, device_id_type=MESH_ID,
        )

    def further(row, way):
        return pltpu.make_async_remote_copy(
            rows(row, 1 + way, way), rows(row, 3, way),
            far_send.at[row, way], far_recv.at[row, way],
            device_id=side[way], device_id_type=MESH_ID,
        )

    def relay(way):
        return pltpu.make_async_remote_copy(
            rows(0, 1 + way, way), rows(1, 1 + way, way),
            own_send.at[1, way, way], own_recv.at[1, way, way],
            device_id=pair, device_id_type=MESH_ID,
        )

    def pass_on(row, way):
        hand(row, way, way).wait_recv()
        further(row, way).start()
        if RELAY and row == 0:
            relay(way).start()

    def cross_on(h):
        cross(h).wait_recv()
        for way in range(2):
            if not (RELAY and way == h):
                hand(1, way, h).start()

    order = ((0, 0, 0), (0, 1, -1), (0, 2, 1), (0, 3, 2), (1, 0, 0), (1, 1, -1), (1, 2, 1), (1, 3, 2))

    def spot(u):
        row, _, dc = order[u]
        return at(dc, row == 1)

    def tables(u):
        here = pl.ds(pl.multiple_of(spot(u) * shard, shard), shard)
        return cos_ref[here, :], sin_ref[here, :]

    def keep(u):
        return pltpu.make_async_copy(
            mine.at[u], kv_ref.at[core, depth, spot(u), near_y], mine_sem.at[u]
        )

    def y_copy(u):
        return pltpu.make_async_remote_copy(
            mine.at[u], kv_ref.at[core, depth, spot(u), near_y],
            y_send.at[u], y_recv.at[u],
            device_id=y_side, device_id_type=MESH_ID,
        )

    def z_copy(u, way, hop, own=True):
        origin = deep(-hop if way == 0 else hop)
        ref = kv_ref.at[core, origin, spot(u)]
        if u in SPLIT:
            ref = kv_ref.at[core, origin, spot(u), near_y]
        elif hop == 3:
            ref = kv_ref.at[core, origin, spot(u), way]
        source = mine.at[u] if u in SPLIT and hop == 0 and own else ref
        return pltpu.make_async_remote_copy(
            source, ref, z_send.at[way, hop, u], z_recv.at[way, hop, u],
            device_id=z_side[way], device_id_type=MESH_ID,
        )

    def z_arrival(u, way, hop):
        origin = deep(-hop - 1 if way == 0 else hop + 1)
        ref = kv_ref.at[core, origin, spot(u)]
        if u in SPLIT:
            ref = kv_ref.at[core, origin, spot(u), near_y]
        elif hop == 3:
            ref = kv_ref.at[core, origin, spot(u), way]
        return pltpu.make_async_remote_copy(
            ref, ref, z_send.at[way, hop, u], z_recv.at[way, hop, u],
            device_id=z_side[way], device_id_type=MESH_ID,
        )

    def core_copy(u, origin, y=None, source=None):
        ref = kv_ref.at[core, origin, spot(u)]
        if y is not None:
            ref = kv_ref.at[core, origin, spot(u), y]
        return pltpu.make_async_remote_copy(
            ref if source is None else source, ref, core_send, core_recv,
            device_id=core_side, device_id_type=MESH_ID,
        )

    def origin_of(stage, way):
        return deep(-stage if way == 0 else stage)

    def y_forward(u, stage, way):
        ref = kv_ref.at[core, origin_of(stage, way), spot(u), near_y]
        return pltpu.make_async_remote_copy(
            ref, ref, fwd_send.at[u, way, stage - 1], fwd_recv.at[u, way, stage - 1],
            device_id=y_side, device_id_type=MESH_ID,
        )

    def y_landed(u, stage, way):
        ref = kv_ref.at[core, origin_of(stage, way), spot(u), 1 - near_y]
        return pltpu.make_async_remote_copy(
            ref, ref, fwd_send.at[u, way, stage - 1], fwd_recv.at[u, way, stage - 1],
            device_id=y_side, device_id_type=MESH_ID,
        )

    def hops(u, stage, way):
        return stage < 3 or (stage == 3 and (u not in SPLIT or way == u % 2))

    def keys(u):
        row, place, _ = order[u]
        y = jnp.dot(tok[row, place], wkv[...], preferred_element_type=jnp.float32)
        cosine, sine = tables(u)
        mine[u, :, :HEAD] = turn(y[:, :HEAD], cosine, sine).astype(jnp.bfloat16)
        mine[u, :, HEAD:] = y[:, HEAD:].astype(jnp.bfloat16)
        keep(u).start()
        y_copy(u).start()

    def ring(u, stage, way):
        if stage == 0:
            if u not in SPLIT:
                keep(u).wait()
                y_copy(u).wait_recv()
            z_copy(u, 0, 0).start()
            z_copy(u, 1, 0).start()
            if u in SPLIT:
                core_copy(u, depth, near_y, mine.at[u]).start()
            else:
                core_copy(u, depth).start()
            return
        z_arrival(u, way, stage - 1).wait_recv()
        if hops(u, stage, way):
            z_copy(u, way, stage, False).start()
        origin = origin_of(stage, way)
        if u in SPLIT:
            y_forward(u, stage, way).start()
            core_copy(u, origin, near_y).start()
        elif stage < 4:
            core_copy(u, origin).start()
        else:
            core_copy(u, origin, way).start()

    def landed(u, stage, way):
        if stage == 0:
            y_copy(u).wait_recv()
            core_copy(u, depth, 1 - near_y).start()
        else:
            y_landed(u, stage, way).wait_recv()
            core_copy(u, origin_of(stage, way), 1 - near_y).start()

    def queries(row, part):
        wide = 2 * HEAD
        x = tok[row].reshape(4 * shard, tok.shape[-1])
        cols = slice(part * wide, (part + 1) * wide)
        y = jnp.dot(x, wq[:, cols], preferred_element_type=jnp.float32)
        for n in range(4):
            u = next(i for i, o in enumerate(order) if o[:2] == (row, n))
            cosine, sine = tables(u)
            here = pl.ds(pl.multiple_of(spot(u) * shard, shard), shard)
            for h in range(2):
                v = y[n * shard : (n + 1) * shard, h * HEAD : (h + 1) * HEAD]
                q_ref[here, part * wide + h * HEAD : part * wide + (h + 1) * HEAD] = turn(
                    v, cosine, sine
                ).astype(jnp.bfloat16)

    def project_keys(u):
        row, place, _ = order[u]
        if u == 0:
            loads[1].wait()
            loads[2].wait()
        elif place == 3:
            further(row, 0).wait_recv()
            further(row, 1).wait_recv()
        elif place:
            hand(row, place - 1, 2 - place).wait_recv()
        keys(u)

    def project_queries(row, part):
        if (row, part) == (0, 0):
            loads[3].wait()
        queries(row, part)

    loads[0].wait()
    for h in range(2):
        hand(0, 0, h).start()
        hand(0, 1, 1 - h).start()
    for h in range(2):
        cross(h).start()
    for kind, *rest in ORDER:
        if kind == 0:
            pass_on(*rest[:2])
        elif kind == 1:
            cross_on(rest[0])
        elif kind == 2:
            project_keys(rest[0])
        elif kind == 3:
            project_queries(*rest[:2])
        elif kind == 4:
            ring(*rest)
        else:
            landed(*rest)

    for h in range(2):
        cross(h).wait_send()
        for row in range(2):
            for way in range(2):
                hand(row, way, h).wait_send()
    for row in range(2):
        for way in range(2):
            further(row, way).wait_send()
    for u in range(len(order)):
        y_copy(u).wait_send()
        if u in SPLIT:
            keep(u).wait()
        for way in range(2):
            for stage in range(4):
                if hops(u, stage, way):
                    z_copy(u, way, stage).wait_send()
            if u in SPLIT:
                for stage in range(1, 5):
                    if hops(u, stage - 1, way):
                        y_forward(u, stage, way).wait_send()
    done = kv_ref.at[core]
    pltpu.make_async_copy(done, done, core_send).wait()
    done = kv_ref.at[1 - core]
    pltpu.make_async_copy(done, done, core_recv).wait()


def gather(tokens, wq, wk, wv, cosine, sine, groups):
    shard, width = tokens.shape
    units = groups
    hbm, vmem = pl.BlockSpec(memory_space=pl.ANY), pl.BlockSpec(memory_space=pltpu.VMEM)
    dma = pltpu.SemaphoreType.DMA
    return pl.pallas_call(
        gather_kernel,
        in_specs=[hbm, hbm, hbm, hbm, vmem, vmem],
        out_specs=[vmem, hbm],
        out_shape=[
            jax.ShapeDtypeStruct((shard * groups, wq.shape[1]), jnp.bfloat16),
            jax.ShapeDtypeStruct((2, Z_RING, groups, 2, shard, 2 * HEAD), jnp.bfloat16),
        ],
        scratch_shapes=[
            pltpu.VMEM((2, RING, shard, width), jnp.bfloat16),
            pltpu.VMEM(wq.shape, jnp.bfloat16),
            pltpu.VMEM((width, 2 * HEAD), jnp.bfloat16),
            pltpu.VMEM((units, shard, 2 * HEAD), jnp.bfloat16),
            dma((4,)),
            dma((2, 3, 2)), dma((2, 3, 2)), dma((2, 2)), dma((2, 2)),
            dma((units,)), dma((units,)), dma((units,)),
            dma((2, 4, units)), dma((2, 4, units)),
            dma((units, 2, 4)), dma((units, 2, 4)),
            dma, dma,
        ],
        compiler_params=pltpu.CompilerParams(collective_id=0, has_side_effects=True),
    )(tokens, wq, wk, wv, cosine, sine)


def body(tokens, w_query, key_weight, value_weight, w_output, block_mask, positions):
    cosine, sine = rotary_tables(positions)
    groups = lax.axis_size("grp")
    q, kv = gather(tokens, w_query, key_weight, value_weight, cosine, sine, groups)
    mixed = attend(block_mask, q, kv)
    return reduce_out(mixed, w_output, groups)


def solution(mesh):
    return jax.shard_map(
        body,
        mesh=mesh,
        in_specs=(
            P(("blk", "grp"), None),
            P(None, "grp"),
            P(None, "grp"),
            P(None, "grp"),
            P("grp", None),
            P("blk", None),
            P("blk"),
        ),
        out_specs=P(("blk", "grp"), None),
        check_vma=False,
    )
```

```python
import functools

import jax
import jax.numpy as jnp
import numpy as np
from jax import lax
from jax.experimental import pallas as pl
from jax.experimental.pallas import tpu as pltpu
from jax.sharding import PartitionSpec as P

HEAD = 128
BLOCK = 128
NEG = -1e30
LOG2E = 1.4426950408889634
SCALE2 = HEAD ** (-0.5) * LOG2E


def inverse_lanes():
    half = HEAD // 2
    inverse = np.power(
        np.float32(500000.0), -(np.float32(2.0) * np.arange(half, dtype=np.float32)) / np.float32(HEAD)
    ).astype(np.float32)
    return jnp.asarray(np.concatenate([inverse, inverse])[None, :])


def turn(v, cosine, sine):
    return v * cosine + pltpu.roll(v, HEAD // 2, 1) * sine


def score(q, k):
    return lax.dot_general(q, k, (((1,), (1,)), ((), ())), preferred_element_type=jnp.float32)


def attend_kernel(
    n_blocks, heads, mask_ref, q_ref, kv_ref, out_ref, near, stream, sem, stream_sem
):
    blk = lax.axis_index("blk")
    rows = q_ref.shape[0] // BLOCK
    shard = kv_ref.shape[4]
    pieces = BLOCK // shard
    lanes = lax.broadcasted_iota(jnp.int32, (1, n_blocks), 1)
    for r in range(rows):
        i = blk * rows + r
        live = mask_ref[r : r + 1, :] != 0
        fixed = (jnp.abs(lanes - i) <= 1) | (lanes < 1)
        left = jnp.where(live & jnp.logical_not(fixed), lanes, n_blocks)
        ids = [0, jnp.maximum(i - 1, 0), i, jnp.minimum(i + 1, n_blocks - 1)]
        last = jnp.int32(-1)
        for _ in range(3):
            last = jnp.min(jnp.where(left > last, left, n_blocks))
            ids.append(jnp.minimum(last, n_blocks - 1))
        for s, j in enumerate(ids):
            owner = j // rows
            for h in range(pieces):
                pltpu.make_async_copy(
                    kv_ref.at[
                        lax.rem(owner, 2),
                        owner // 4,
                        lax.rem(j, rows) * pieces + h,
                        lax.rem(owner // 2, 2),
                    ],
                    near.at[r, pl.ds(s * BLOCK + h * shard, shard)],
                    sem.at[r],
                ).start()

    def queries(r):
        return jnp.concatenate(
            [
                q_ref[r * BLOCK : (r + 1) * BLOCK, h * HEAD : (h + 1) * HEAD]
                for h in range(heads)
            ],
            axis=0,
        )

    def put(r, mixed):
        for h in range(heads):
            out_ref[r * BLOCK : (r + 1) * BLOCK, h * HEAD : (h + 1) * HEAD] = mixed[
                h * BLOCK : (h + 1) * BLOCK
            ].astype(jnp.bfloat16)

    def near_row(r):
        i = blk * rows + r
        s = score(queries(r), near[r, :, :HEAD])
        parts = [
            jnp.where(i == 1, NEG, s[:, :BLOCK]),
            s[:, BLOCK : 3 * BLOCK],
            jnp.where(i == n_blocks - 1, NEG, s[:, 3 * BLOCK : 4 * BLOCK]),
            s[:, 4 * BLOCK :],
        ]
        s = jnp.concatenate(parts, axis=1)
        top = jnp.max(s, axis=1, keepdims=True)
        p = jnp.exp2(s * SCALE2 - top * SCALE2)
        total = jnp.sum(p, axis=1, keepdims=True)
        mixed = jnp.dot(
            p.astype(jnp.bfloat16), near[r, :, HEAD:], preferred_element_type=jnp.float32
        )
        put(r, mixed / total)

    for r in range(rows):
        pltpu.make_async_copy(near.at[r], near.at[r], sem.at[r]).wait()
        if r:
            near_row(r)

    @pl.when(blk != 0)
    def _():
        near_row(0)

    @pl.when(blk == 0)
    def _():
        steps = kv_ref.shape[0] * kv_ref.shape[1]

        def fetch(step, slot):
            return pltpu.make_async_copy(
                kv_ref.at[step // kv_ref.shape[1], lax.rem(step, kv_ref.shape[1])],
                stream.at[slot],
                stream_sem.at[slot],
            )

        fetch(0, 0).start()
        q = queries(0)
        n = q.shape[0]

        def body(step, state):
            top, total, accum = state
            slot = lax.rem(step, 2)
            fetch(step, slot).wait()

            @pl.when(step + 1 < steps)
            def _():
                fetch(step + 1, 1 - slot).start()

            both = stream[slot].reshape(-1, 2 * HEAD)
            s = score(q, both[:, :HEAD])
            new = jnp.maximum(top, jnp.max(s, axis=1, keepdims=True))
            p = jnp.exp2(s * SCALE2 - new * SCALE2)
            factor = jnp.exp2((top - new) * SCALE2)
            total = total * factor + jnp.sum(p, axis=1, keepdims=True)
            accum = accum * factor + jnp.dot(
                p.astype(jnp.bfloat16),
                both[:, HEAD:],
                preferred_element_type=jnp.float32,
            )
            return new, total, accum

        top, total, accum = lax.fori_loop(
            0,
            steps,
            body,
            (
                jnp.full((n, 1), NEG, jnp.float32),
                jnp.zeros((n, 1), jnp.float32),
                jnp.zeros((n, HEAD), jnp.float32),
            ),
        )
        put(0, accum / total)


def attend(block_mask, q, kv):
    rows = q.shape[0] // BLOCK
    n_blocks = block_mask.shape[1]
    heads = q.shape[1] // HEAD
    vmem = pl.BlockSpec(memory_space=pltpu.VMEM)
    return pl.pallas_call(
        functools.partial(attend_kernel, n_blocks, heads),
        in_specs=[vmem, vmem, pl.BlockSpec(memory_space=pl.ANY)],
        out_specs=vmem,
        out_shape=jax.ShapeDtypeStruct(q.shape, jnp.bfloat16),
        scratch_shapes=[
            pltpu.VMEM((rows, 7 * BLOCK, 2 * HEAD), jnp.bfloat16),
            pltpu.VMEM((2, *kv.shape[2:]), jnp.bfloat16),
            pltpu.SemaphoreType.DMA((rows,)),
            pltpu.SemaphoreType.DMA((2,)),
        ],
    )(block_mask, q, kv)


MESH_ID = pl.DeviceIdType.MESH
RING = 4
HALVES = 2


def places():
    g = lax.axis_index("grp")
    col, row = lax.rem(g, RING), g // RING

    def at(dc, flip):
        r = 1 - row if flip else row
        return r * RING + lax.rem(col + dc + RING, RING)

    return at


def greet(peers):
    barrier = pltpu.get_barrier_semaphore()
    for peer in peers:
        pl.semaphore_signal(barrier, inc=1, device_id=peer, device_id_type=MESH_ID)
    pl.semaphore_wait(barrier, len(peers))


def reduce_kernel(
    shard, mixed_ref, w_ref, out_ref,
    terms, far_in, near_in, pair_out, pair_in, relay_in,
    far_send, far_recv, near_send, near_recv, pair_send, pair_recv, relay_send, relay_recv,
):
    at = places()
    right, left, pair = at(1, False), at(-1, False), at(0, True)
    side = ({"grp": right}, {"grp": left})
    width = w_ref.shape[1] // HALVES
    FAR, RIGHT, LEFT, OWN = 0, 1, 2, 3
    greet([side[0], side[1], {"grp": pair}])

    def product(slot, dc):
        lhs = jnp.concatenate(
            [
                mixed_ref[pl.ds(pl.multiple_of(at(dc, flip) * shard, shard), shard), :]
                for flip in (True, False)
            ],
            axis=0,
        )
        step = 512
        for half in range(HALVES):
            for c in range(width // step):
                cols = slice(c * step, (c + 1) * step)
                wide = slice(half * width + c * step, half * width + (c + 1) * step)
                t = jnp.dot(lhs, w_ref[:, wide], preferred_element_type=jnp.float32)
                for row in range(2):
                    terms[slot, row, half, :, cols] = t[
                        row * shard : (row + 1) * shard
                    ].astype(jnp.bfloat16)

    def far(row, way):
        return pltpu.make_async_remote_copy(
            terms.at[FAR, row, way], far_in.at[way, row],
            far_send.at[way, row], far_recv.at[way, row],
            device_id=side[way], device_id_type=MESH_ID,
        )

    def near(row, way, half):
        return pltpu.make_async_remote_copy(
            terms.at[RIGHT + way, row, half], near_in.at[way, row, half],
            near_send.at[way, row, half], near_recv.at[way, row, half],
            device_id=side[way], device_id_type=MESH_ID,
        )

    def across(half):
        return pltpu.make_async_remote_copy(
            pair_out.at[half], pair_in.at[half], pair_send.at[half], pair_recv.at[half],
            device_id={"grp": pair}, device_id_type=MESH_ID,
        )

    def relay(way):
        return pltpu.make_async_remote_copy(
            terms.at[RIGHT + way, 0, 1 - way], relay_in.at[way],
            relay_send.at[way], relay_recv.at[way],
            device_id={"grp": pair}, device_id_type=MESH_ID,
        )

    def take(way):
        relay(way).wait_recv()
        slot = RIGHT + way
        terms[slot, 1, 1 - way] = (
            terms[slot, 1, 1 - way].astype(jnp.float32) + relay_in[way].astype(jnp.float32)
        ).astype(jnp.bfloat16)
        near(1, way, 1 - way).start()

    def carry(row, way):
        far(row, way).wait_recv()
        slot = RIGHT + way
        terms[slot, row, way] = (
            terms[slot, row, way].astype(jnp.float32) + far_in[way, row].astype(jnp.float32)
        ).astype(jnp.bfloat16)
        near(row, way, way).start()

    def gathered(row, half):
        total = terms[OWN, row, half].astype(jnp.float32)
        for way in range(2):
            if row == 1 or way == half:
                near(row, way, half).wait_recv()
                total = total + near_in[way, row, half].astype(jnp.float32)
        return total

    product(FAR, 2)
    far(0, 0).start()
    far(0, 1).start()
    product(RIGHT, 1)
    relay(0).start()
    product(LEFT, -1)
    relay(1).start()
    carry(0, 0)
    carry(0, 1)
    far(1, 0).start()
    far(1, 1).start()
    product(OWN, 0)
    take(0)
    take(1)
    for half in range(HALVES):
        pair_out[half] = gathered(0, half).astype(jnp.bfloat16)
        across(half).start()
    carry(1, 0)
    carry(1, 1)
    for half in range(HALVES):
        total = gathered(1, half)
        across(half).wait_recv()
        total = total + pair_in[half].astype(jnp.float32)
        out_ref[:, half * width : (half + 1) * width] = total.astype(jnp.bfloat16)
    for row in range(2):
        for way in range(2):
            far(row, way).wait_send()
            for half in range(HALVES):
                if row == 1 or way == half:
                    near(row, way, half).wait_send()
    for way in range(2):
        relay(way).wait_send()
    for half in range(HALVES):
        across(half).wait_send()


def reduce_out(mixed, w_output, groups):
    rows, width = mixed.shape[0], w_output.shape[1]
    shard, half = rows // groups, width // HALVES
    vmem = pl.BlockSpec(memory_space=pltpu.VMEM)
    dma = pltpu.SemaphoreType.DMA
    piece = (shard, half)
    return pl.pallas_call(
        functools.partial(reduce_kernel, shard),
        in_specs=[vmem, vmem],
        out_specs=vmem,
        out_shape=jax.ShapeDtypeStruct((shard, width), jnp.bfloat16),
        scratch_shapes=[
            pltpu.VMEM((4, 2, HALVES, *piece), jnp.bfloat16),
            pltpu.VMEM((2, 2, *piece), jnp.bfloat16),
            pltpu.VMEM((2, 2, HALVES, *piece), jnp.bfloat16),
            pltpu.VMEM((HALVES, *piece), jnp.bfloat16),
            pltpu.VMEM((HALVES, *piece), jnp.bfloat16),
            pltpu.VMEM((2, *piece), jnp.bfloat16),
            dma((2, 2)), dma((2, 2)),
            dma((2, 2, HALVES)), dma((2, 2, HALVES)),
            dma((HALVES,)), dma((HALVES,)),
            dma((2,)), dma((2,)),
        ],
        compiler_params=pltpu.CompilerParams(collective_id=1, has_side_effects=True),
    )(mixed, w_output)


Z_RING = 8
RELAY = False
SPLIT = (0, 3, 4, 5, 7)
ORDER = (
    (2, 0, 0, 0), (4, 0, 0, 0), (5, 0, 0, 0), (4, 0, 1, 0), (4, 0, 1, 1), (0, 0, 0, 0),
    (0, 0, 1, 0), (1, 0, 0, 0), (4, 0, 2, 0), (4, 0, 2, 1), (5, 0, 1, 0), (5, 0, 1, 1),
    (4, 0, 3, 0), (2, 1, 0, 0), (1, 1, 0, 0), (2, 2, 0, 0), (2, 4, 0, 0), (4, 4, 0, 0),
    (2, 3, 0, 0), (4, 3, 0, 0), (4, 2, 0, 0), (4, 1, 0, 0), (4, 0, 3, 1), (4, 0, 4, 0),
    (5, 0, 2, 0), (5, 0, 2, 1), (5, 0, 3, 0), (4, 4, 1, 0), (4, 4, 1, 1), (5, 4, 0, 0),
    (3, 0, 0, 0), (0, 1, 0, 0), (4, 3, 1, 0), (4, 3, 1, 1), (5, 0, 3, 1), (5, 3, 0, 0),
    (3, 0, 1, 0), (4, 2, 1, 0), (4, 2, 1, 1), (4, 1, 1, 0), (4, 1, 1, 1), (4, 4, 2, 0),
    (4, 4, 2, 1), (5, 0, 4, 0), (4, 3, 2, 0), (4, 3, 2, 1), (5, 3, 1, 0), (0, 1, 1, 0),
    (2, 5, 0, 0), (2, 6, 0, 0), (4, 5, 0, 0), (4, 2, 2, 0), (4, 2, 2, 1), (4, 1, 2, 0),
    (4, 4, 3, 0), (4, 4, 3, 1), (4, 1, 2, 1), (4, 3, 3, 0), (4, 3, 3, 1), (5, 3, 1, 1),
    (5, 3, 2, 0), (5, 3, 2, 1), (5, 4, 1, 0), (5, 4, 1, 1), (5, 4, 2, 0), (5, 4, 2, 1),
    (5, 5, 0, 0), (4, 6, 0, 0), (4, 5, 1, 0), (4, 5, 1, 1), (5, 4, 3, 0), (2, 7, 0, 0),
    (4, 7, 0, 0), (4, 2, 3, 0), (4, 2, 3, 1), (4, 1, 3, 0), (4, 4, 4, 0), (4, 3, 4, 1),
    (4, 1, 3, 1), (5, 3, 3, 0), (5, 3, 3, 1), (5, 4, 3, 1), (5, 5, 1, 0), (3, 1, 0, 0),
    (4, 6, 1, 0), (4, 7, 1, 0), (4, 7, 1, 1), (4, 6, 1, 1), (4, 5, 2, 0), (4, 5, 2, 1),
    (4, 2, 4, 0), (4, 2, 4, 1), (4, 1, 4, 0), (4, 1, 4, 1), (5, 3, 4, 1), (5, 4, 4, 0),
    (5, 5, 1, 1), (5, 7, 0, 0), (3, 1, 1, 0), (4, 7, 2, 1), (4, 6, 2, 0), (5, 7, 1, 0),
    (5, 7, 1, 1), (4, 7, 2, 0), (5, 5, 2, 0), (4, 6, 2, 1), (4, 5, 3, 0), (5, 5, 2, 1),
    (4, 5, 3, 1), (4, 7, 3, 1), (5, 7, 2, 1), (4, 6, 3, 0), (5, 7, 2, 0), (4, 7, 3, 0),
    (5, 5, 3, 0), (4, 6, 3, 1), (5, 5, 3, 1), (4, 5, 4, 1), (4, 7, 4, 1), (5, 7, 3, 1),
    (4, 6, 4, 0), (5, 7, 3, 0), (4, 6, 4, 1), (5, 5, 4, 1), (5, 7, 4, 1),
)


def gather_kernel(
    tokens_ref, wq_ref, wk_ref, wv_ref, pos_ref, inv_ref, q_ref, kv_ref,
    cos_ref, sin_ref, tok, wq, wkv, mine,
    load_sem, own_send, own_recv, far_send, far_recv,
    mine_sem, y_send, y_recv, z_send, z_recv, fwd_send, fwd_recv, core_send, core_recv,
):
    at = places()
    side = ({"grp": at(1, False)}, {"grp": at(-1, False)})
    pair = {"grp": at(0, True)}
    blk = lax.axis_index("blk")
    core, near_y, depth = lax.rem(blk, 2), lax.rem(blk // 2, 2), blk // 4
    shard, half = tokens_ref.shape[0], tokens_ref.shape[0] // 2

    def deep(step):
        return lax.rem(depth + step + Z_RING, Z_RING)

    z_side = tuple({"blk": (deep(d) * 2 + near_y) * 2 + core} for d in (1, -1))
    y_side = {"blk": (depth * 2 + 1 - near_y) * 2 + core}
    core_side = {"blk": (depth * 2 + near_y) * 2 + 1 - core}

    loads = [
        pltpu.make_async_copy(tokens_ref, tok.at[0, 0], load_sem.at[0]),
        pltpu.make_async_copy(wk_ref, wkv.at[:, pl.ds(0, HEAD)], load_sem.at[1]),
        pltpu.make_async_copy(wv_ref, wkv.at[:, pl.ds(HEAD, HEAD)], load_sem.at[2]),
        pltpu.make_async_copy(wq_ref, wq, load_sem.at[3]),
    ]
    for load in loads:
        load.start()
    greet([*side, pair, *z_side, y_side, core_side])

    def rows(row, place, h):
        return tok.at[row, place, pl.ds(h * half, half)]

    def hand(row, way, h):
        return pltpu.make_async_remote_copy(
            rows(row, 0, h), rows(row, 1 + way, h),
            own_send.at[row, way, h], own_recv.at[row, way, h],
            device_id=side[way], device_id_type=MESH_ID,
        )

    def cross(h):
        return pltpu.make_async_remote_copy(
            rows(0, 0, h), rows(1, 0, h), own_send.at[0, 2, h], own_recv.at[0, 2, h],
            device_id=pair, device_id_type=MESH_ID,
        )

    def further(row, way):
        return pltpu.make_async_remote_copy(
            rows(row, 1 + way, way), rows(row, 3, way),
            far_send.at[row, way], far_recv.at[row, way],
            device_id=side[way], device_id_type=MESH_ID,
        )

    def relay(way):
        return pltpu.make_async_remote_copy(
            rows(0, 1 + way, way), rows(1, 1 + way, way),
            own_send.at[1, way, way], own_recv.at[1, way, way],
            device_id=pair, device_id_type=MESH_ID,
        )

    def pass_on(row, way):
        hand(row, way, way).wait_recv()
        further(row, way).start()
        if RELAY and row == 0:
            relay(way).start()

    def cross_on(h):
        cross(h).wait_recv()
        for way in range(2):
            if not (RELAY and way == h):
                hand(1, way, h).start()

    order = ((0, 0, 0), (0, 1, -1), (0, 2, 1), (0, 3, 2), (1, 0, 0), (1, 1, -1), (1, 2, 1), (1, 3, 2))

    def spot(u):
        row, _, dc = order[u]
        return at(dc, row == 1)

    def tables(u):
        here = pl.ds(pl.multiple_of(spot(u) * shard, shard), shard)
        return cos_ref[here, :], sin_ref[here, :]

    def keep(u):
        return pltpu.make_async_copy(
            mine.at[u], kv_ref.at[core, depth, spot(u), near_y], mine_sem.at[u]
        )

    def y_copy(u):
        return pltpu.make_async_remote_copy(
            mine.at[u], kv_ref.at[core, depth, spot(u), near_y],
            y_send.at[u], y_recv.at[u],
            device_id=y_side, device_id_type=MESH_ID,
        )

    def z_copy(u, way, hop, own=True):
        origin = deep(-hop if way == 0 else hop)
        ref = kv_ref.at[core, origin, spot(u)]
        if u in SPLIT:
            ref = kv_ref.at[core, origin, spot(u), near_y]
        elif hop == 3:
            ref = kv_ref.at[core, origin, spot(u), way]
        source = mine.at[u] if u in SPLIT and hop == 0 and own else ref
        return pltpu.make_async_remote_copy(
            source, ref, z_send.at[way, hop, u], z_recv.at[way, hop, u],
            device_id=z_side[way], device_id_type=MESH_ID,
        )

    def z_arrival(u, way, hop):
        origin = deep(-hop - 1 if way == 0 else hop + 1)
        ref = kv_ref.at[core, origin, spot(u)]
        if u in SPLIT:
            ref = kv_ref.at[core, origin, spot(u), near_y]
        elif hop == 3:
            ref = kv_ref.at[core, origin, spot(u), way]
        return pltpu.make_async_remote_copy(
            ref, ref, z_send.at[way, hop, u], z_recv.at[way, hop, u],
            device_id=z_side[way], device_id_type=MESH_ID,
        )

    def core_copy(u, origin, y=None, source=None):
        ref = kv_ref.at[core, origin, spot(u)]
        if y is not None:
            ref = kv_ref.at[core, origin, spot(u), y]
        return pltpu.make_async_remote_copy(
            ref if source is None else source, ref, core_send, core_recv,
            device_id=core_side, device_id_type=MESH_ID,
        )

    def origin_of(stage, way):
        return deep(-stage if way == 0 else stage)

    def y_forward(u, stage, way):
        ref = kv_ref.at[core, origin_of(stage, way), spot(u), near_y]
        return pltpu.make_async_remote_copy(
            ref, ref, fwd_send.at[u, way, stage - 1], fwd_recv.at[u, way, stage - 1],
            device_id=y_side, device_id_type=MESH_ID,
        )

    def y_landed(u, stage, way):
        ref = kv_ref.at[core, origin_of(stage, way), spot(u), 1 - near_y]
        return pltpu.make_async_remote_copy(
            ref, ref, fwd_send.at[u, way, stage - 1], fwd_recv.at[u, way, stage - 1],
            device_id=y_side, device_id_type=MESH_ID,
        )

    def hops(u, stage, way):
        return stage < 3 or (stage == 3 and (u not in SPLIT or way == u % 2))

    def keys(u):
        row, place, _ = order[u]
        y = jnp.dot(tok[row, place], wkv[...], preferred_element_type=jnp.float32)
        cosine, sine = tables(u)
        mine[u, :, :HEAD] = turn(y[:, :HEAD], cosine, sine).astype(jnp.bfloat16)
        mine[u, :, HEAD:] = y[:, HEAD:].astype(jnp.bfloat16)
        keep(u).start()
        y_copy(u).start()

    def ring(u, stage, way):
        if stage == 0:
            if u not in SPLIT:
                keep(u).wait()
                y_copy(u).wait_recv()
            z_copy(u, 0, 0).start()
            z_copy(u, 1, 0).start()
            if u in SPLIT:
                core_copy(u, depth, near_y, mine.at[u]).start()
            else:
                core_copy(u, depth).start()
            return
        z_arrival(u, way, stage - 1).wait_recv()
        if hops(u, stage, way):
            z_copy(u, way, stage, False).start()
        origin = origin_of(stage, way)
        if u in SPLIT:
            y_forward(u, stage, way).start()
            core_copy(u, origin, near_y).start()
        elif stage < 4:
            core_copy(u, origin).start()
        else:
            core_copy(u, origin, way).start()

    def landed(u, stage, way):
        if stage == 0:
            y_copy(u).wait_recv()
            core_copy(u, depth, 1 - near_y).start()
        else:
            y_landed(u, stage, way).wait_recv()
            core_copy(u, origin_of(stage, way), 1 - near_y).start()

    def queries(row, part):
        wide = 2 * HEAD
        x = tok[row].reshape(4 * shard, tok.shape[-1])
        cols = slice(part * wide, (part + 1) * wide)
        y = jnp.dot(x, wq[:, cols], preferred_element_type=jnp.float32)
        for n in range(4):
            u = next(i for i, o in enumerate(order) if o[:2] == (row, n))
            cosine, sine = tables(u)
            here = pl.ds(pl.multiple_of(spot(u) * shard, shard), shard)
            for h in range(2):
                v = y[n * shard : (n + 1) * shard, h * HEAD : (h + 1) * HEAD]
                q_ref[here, part * wide + h * HEAD : part * wide + (h + 1) * HEAD] = turn(
                    v, cosine, sine
                ).astype(jnp.bfloat16)

    def project_keys(u):
        row, place, _ = order[u]
        if u == 0:
            loads[1].wait()
            loads[2].wait()
        elif place == 3:
            further(row, 0).wait_recv()
            further(row, 1).wait_recv()
        elif place:
            hand(row, place - 1, 2 - place).wait_recv()
        keys(u)

    def project_queries(row, part):
        if (row, part) == (0, 0):
            loads[3].wait()
        queries(row, part)

    loads[0].wait()
    for h in range(2):
        hand(0, 0, h).start()
        hand(0, 1, 1 - h).start()
    for h in range(2):
        cross(h).start()
    lanes = lax.broadcasted_iota(jnp.int32, (1, HEAD), 1)
    flip = jnp.where(lanes < HEAD // 2, -1.0, 1.0)

    @pl.loop(0, pos_ref.shape[0])
    def _(step):
        here = pl.ds(pl.multiple_of(step * HEAD, HEAD), HEAD)
        spread = jnp.broadcast_to(pos_ref[pl.ds(step, 1), :].astype(jnp.float32), (HEAD, HEAD))
        angles = spread.T * inv_ref[...]
        cos_ref[here, :] = jnp.cos(angles)
        sin_ref[here, :] = jnp.sin(angles) * flip

    for kind, *rest in ORDER:
        if kind == 0:
            pass_on(*rest[:2])
        elif kind == 1:
            cross_on(rest[0])
        elif kind == 2:
            project_keys(rest[0])
        elif kind == 3:
            project_queries(*rest[:2])
        elif kind == 4:
            ring(*rest)
        else:
            landed(*rest)

    for h in range(2):
        cross(h).wait_send()
        for row in range(2):
            for way in range(2):
                hand(row, way, h).wait_send()
    for row in range(2):
        for way in range(2):
            further(row, way).wait_send()
    for u in range(len(order)):
        y_copy(u).wait_send()
        if u in SPLIT:
            keep(u).wait()
        for way in range(2):
            for stage in range(4):
                if hops(u, stage, way):
                    z_copy(u, way, stage).wait_send()
            if u in SPLIT:
                for stage in range(1, 5):
                    if hops(u, stage - 1, way):
                        y_forward(u, stage, way).wait_send()
    done = kv_ref.at[core]
    pltpu.make_async_copy(done, done, core_send).wait()
    done = kv_ref.at[1 - core]
    pltpu.make_async_copy(done, done, core_recv).wait()


def gather(tokens, wq, wk, wv, positions, groups):
    shard, width = tokens.shape
    units = groups
    hbm, vmem = pl.BlockSpec(memory_space=pl.ANY), pl.BlockSpec(memory_space=pltpu.VMEM)
    dma = pltpu.SemaphoreType.DMA
    return pl.pallas_call(
        gather_kernel,
        in_specs=[hbm, hbm, hbm, hbm, vmem, vmem],
        out_specs=[vmem, hbm],
        out_shape=[
            jax.ShapeDtypeStruct((shard * groups, wq.shape[1]), jnp.bfloat16),
            jax.ShapeDtypeStruct((2, Z_RING, groups, 2, shard, 2 * HEAD), jnp.bfloat16),
        ],
        scratch_shapes=[
            pltpu.VMEM((shard * groups, HEAD), jnp.float32),
            pltpu.VMEM((shard * groups, HEAD), jnp.float32),
            pltpu.VMEM((2, RING, shard, width), jnp.bfloat16),
            pltpu.VMEM(wq.shape, jnp.bfloat16),
            pltpu.VMEM((width, 2 * HEAD), jnp.bfloat16),
            pltpu.VMEM((units, shard, 2 * HEAD), jnp.bfloat16),
            dma((4,)),
            dma((2, 3, 2)), dma((2, 3, 2)), dma((2, 2)), dma((2, 2)),
            dma((units,)), dma((units,)), dma((units,)),
            dma((2, 4, units)), dma((2, 4, units)),
            dma((units, 2, 4)), dma((units, 2, 4)),
            dma, dma,
        ],
        compiler_params=pltpu.CompilerParams(collective_id=0, has_side_effects=True),
    )(tokens, wq, wk, wv, positions.reshape(-1, HEAD), inverse_lanes())


def body(tokens, w_query, key_weight, value_weight, w_output, block_mask, positions):
    groups = lax.axis_size("grp")
    q, kv = gather(tokens, w_query, key_weight, value_weight, positions, groups)
    mixed = attend(block_mask, q, kv)
    return reduce_out(mixed, w_output, groups)


def solution(mesh):
    return jax.shard_map(
        body,
        mesh=mesh,
        in_specs=(
            P(("blk", "grp"), None),
            P(None, "grp"),
            P(None, "grp"),
            P(None, "grp"),
            P("grp", None),
            P("blk", None),
            P("blk"),
        ),
        out_specs=P(("blk", "grp"), None),
        check_vma=False,
    )
```

```python
import functools

import jax
import jax.numpy as jnp
import numpy as np
from jax import lax
from jax.experimental import pallas as pl
from jax.experimental.pallas import tpu as pltpu
from jax.sharding import PartitionSpec as P

HEAD = 128
BLOCK = 128
NEG = -1e30
LOG2E = 1.4426950408889634
SCALE2 = HEAD ** (-0.5) * LOG2E


def inverse_lanes():
    half = HEAD // 2
    inverse = np.power(
        np.float32(500000.0), -(np.float32(2.0) * np.arange(half, dtype=np.float32)) / np.float32(HEAD)
    ).astype(np.float32)
    return jnp.asarray(np.concatenate([inverse, inverse])[None, :])


def turn(v, cosine, sine):
    return v * cosine + pltpu.roll(v, HEAD // 2, 1) * sine


def score(q, k):
    return lax.dot_general(q, k, (((1,), (1,)), ((), ())), preferred_element_type=jnp.float32)


def attend_kernel(
    n_blocks, heads, mask_ref, q_ref, kv_ref, out_ref, near, stream, ahead, sem, stream_sem
):
    blk = lax.axis_index("blk")
    rows = q_ref.shape[0] // BLOCK
    shard = kv_ref.shape[4]
    pieces = BLOCK // shard
    lanes = lax.broadcasted_iota(jnp.int32, (1, n_blocks), 1)
    for r in range(rows):
        i = blk * rows + r
        live = mask_ref[r : r + 1, :] != 0
        fixed = (jnp.abs(lanes - i) <= 1) | (lanes < 1)
        left = jnp.where(live & jnp.logical_not(fixed), lanes, n_blocks)
        ids = [0, jnp.maximum(i - 1, 0), i, jnp.minimum(i + 1, n_blocks - 1)]
        last = jnp.int32(-1)
        for _ in range(3):
            last = jnp.min(jnp.where(left > last, left, n_blocks))
            ids.append(jnp.minimum(last, n_blocks - 1))
        for s, j in enumerate(ids):
            owner = j // rows
            for h in range(pieces):
                pltpu.make_async_copy(
                    kv_ref.at[
                        lax.rem(owner, 2),
                        owner // 4,
                        lax.rem(j, rows) * pieces + h,
                        lax.rem(owner // 2, 2),
                    ],
                    near.at[r, pl.ds(s * BLOCK + h * shard, shard)],
                    sem.at[r],
                ).start()

    def queries(r):
        return jnp.concatenate(
            [
                q_ref[r * BLOCK : (r + 1) * BLOCK, h * HEAD : (h + 1) * HEAD]
                for h in range(heads)
            ],
            axis=0,
        )

    def put(r, mixed):
        for h in range(heads):
            out_ref[r * BLOCK : (r + 1) * BLOCK, h * HEAD : (h + 1) * HEAD] = mixed[
                h * BLOCK : (h + 1) * BLOCK
            ].astype(jnp.bfloat16)

    def near_row(r):
        i = blk * rows + r
        s = score(queries(r), near[r, :, :HEAD])
        parts = [
            jnp.where(i == 1, NEG, s[:, :BLOCK]),
            s[:, BLOCK : 3 * BLOCK],
            jnp.where(i == n_blocks - 1, NEG, s[:, 3 * BLOCK : 4 * BLOCK]),
            s[:, 4 * BLOCK :],
        ]
        s = jnp.concatenate(parts, axis=1)
        top = jnp.max(s, axis=1, keepdims=True)
        p = jnp.exp2(s * SCALE2 - top * SCALE2)
        total = jnp.sum(p, axis=1, keepdims=True)
        mixed = jnp.dot(
            p.astype(jnp.bfloat16), near[r, :, HEAD:], preferred_element_type=jnp.float32
        )
        put(r, mixed / total)

    for r in range(rows):
        pltpu.make_async_copy(near.at[r], near.at[r], sem.at[r]).wait()
        if r:
            near_row(r)

    @pl.when(blk != 0)
    def _():
        near_row(0)

    @pl.when(blk == 0)
    def _():
        steps = kv_ref.shape[0] * kv_ref.shape[1]

        def fetch(step, slot):
            return pltpu.make_async_copy(
                kv_ref.at[step // kv_ref.shape[1], lax.rem(step, kv_ref.shape[1])],
                stream.at[slot],
                stream_sem.at[slot],
            )

        q = queries(0)
        n = q.shape[0]
        for step in range(steps):
            fetch(step, step).start()

        def keys_of(step):
            return stream[step].reshape(-1, 2 * HEAD)

        def fold(s, both, state):
            top, total, accum = state
            new = jnp.maximum(top, jnp.max(s, axis=1, keepdims=True))
            p = jnp.exp2(s * SCALE2 - new * SCALE2)
            factor = jnp.exp2((top - new) * SCALE2)
            total = total * factor + jnp.sum(p, axis=1, keepdims=True)
            accum = accum * factor + jnp.dot(
                p.astype(jnp.bfloat16), both[:, HEAD:], preferred_element_type=jnp.float32
            )
            return new, total, accum

        fetch(0, 0).wait()
        ahead[0] = score(q, keys_of(0)[:, :HEAD])

        def body(pair, state):
            first = pair * 2
            after = jnp.minimum(first + 2, steps - 1)
            fetch(first + 1, first + 1).wait()

            @pl.when(first + 2 < steps)
            def _():
                fetch(after, after).wait()

            ahead[1] = score(q, keys_of(first + 1)[:, :HEAD])
            state = fold(ahead[0], keys_of(first), state)
            ahead[0] = score(q, keys_of(after)[:, :HEAD])
            return fold(ahead[1], keys_of(first + 1), state)

        top, total, accum = lax.fori_loop(
            0,
            steps // 2,
            body,
            (
                jnp.full((n, 1), NEG, jnp.float32),
                jnp.zeros((n, 1), jnp.float32),
                jnp.zeros((n, HEAD), jnp.float32),
            ),
        )
        put(0, accum / total)


def attend(block_mask, q, kv):
    rows = q.shape[0] // BLOCK
    n_blocks = block_mask.shape[1]
    heads = q.shape[1] // HEAD
    vmem = pl.BlockSpec(memory_space=pltpu.VMEM)
    return pl.pallas_call(
        functools.partial(attend_kernel, n_blocks, heads),
        in_specs=[vmem, vmem, pl.BlockSpec(memory_space=pl.ANY)],
        out_specs=vmem,
        out_shape=jax.ShapeDtypeStruct(q.shape, jnp.bfloat16),
        scratch_shapes=[
            pltpu.VMEM((rows, 7 * BLOCK, 2 * HEAD), jnp.bfloat16),
            pltpu.VMEM((16, *kv.shape[2:]), jnp.bfloat16),
            pltpu.VMEM((2, heads * BLOCK, 1024), jnp.float32),
            pltpu.SemaphoreType.DMA((rows,)),
            pltpu.SemaphoreType.DMA((16,)),
        ],
    )(block_mask, q, kv)


MESH_ID = pl.DeviceIdType.MESH
RING = 4
HALVES = 2


def places():
    g = lax.axis_index("grp")
    col, row = lax.rem(g, RING), g // RING

    def at(dc, flip):
        r = 1 - row if flip else row
        return r * RING + lax.rem(col + dc + RING, RING)

    return at


def greet(peers):
    barrier = pltpu.get_barrier_semaphore()
    for peer in peers:
        pl.semaphore_signal(barrier, inc=1, device_id=peer, device_id_type=MESH_ID)
    pl.semaphore_wait(barrier, len(peers))


GROUPS = 2


def reduce_kernel(
    shard, mixed_ref, w_ref, out_ref,
    terms, far_in, near_in, pair_out, pair_in, relay_in,
    far_send, far_recv, near_send, near_recv, pair_send, pair_recv, relay_send, relay_recv,
):
    at = places()
    right, left, pair = at(1, False), at(-1, False), at(0, True)
    side = ({"grp": right}, {"grp": left})
    width = w_ref.shape[1] // (GROUPS * HALVES)
    FAR, RIGHT, LEFT, OWN = 0, 1, 2, 3
    greet([side[0], side[1], {"grp": pair}])

    def product(slot, dc, g):
        lhs = jnp.concatenate(
            [
                mixed_ref[pl.ds(pl.multiple_of(at(dc, flip) * shard, shard), shard), :]
                for flip in (True, False)
            ],
            axis=0,
        )
        step = 512
        for half in range(HALVES):
            for c in range(width // step):
                cols = slice(c * step, (c + 1) * step)
                first = (g * HALVES + half) * width + c * step
                t = jnp.dot(
                    lhs, w_ref[:, first : first + step], preferred_element_type=jnp.float32
                )
                for row in range(2):
                    terms[g, slot, row, half, :, cols] = t[
                        row * shard : (row + 1) * shard
                    ].astype(jnp.bfloat16)

    def far(row, way, g):
        return pltpu.make_async_remote_copy(
            terms.at[g, FAR, row, way], far_in.at[g, way, row],
            far_send.at[g, way, row], far_recv.at[g, way, row],
            device_id=side[way], device_id_type=MESH_ID,
        )

    def near(row, way, half, g):
        return pltpu.make_async_remote_copy(
            terms.at[g, RIGHT + way, row, half], near_in.at[g, way, row, half],
            near_send.at[g, way, row, half], near_recv.at[g, way, row, half],
            device_id=side[way], device_id_type=MESH_ID,
        )

    def across(half, g):
        return pltpu.make_async_remote_copy(
            pair_out.at[g, half], pair_in.at[g, half],
            pair_send.at[g, half], pair_recv.at[g, half],
            device_id={"grp": pair}, device_id_type=MESH_ID,
        )

    def relay(way, g):
        return pltpu.make_async_remote_copy(
            terms.at[g, RIGHT + way, 0, 1 - way], relay_in.at[g, way],
            relay_send.at[g, way], relay_recv.at[g, way],
            device_id={"grp": pair}, device_id_type=MESH_ID,
        )

    def join(slot, row, half, g, more):
        terms[g, slot, row, half] = (
            terms[g, slot, row, half].astype(jnp.float32) + more.astype(jnp.float32)
        ).astype(jnp.bfloat16)

    def take(way, g):
        relay(way, g).wait_recv()
        join(RIGHT + way, 1, 1 - way, g, relay_in[g, way])
        near(1, way, 1 - way, g).start()

    def carry(row, way, g):
        far(row, way, g).wait_recv()
        join(RIGHT + way, row, way, g, far_in[g, way, row])
        near(row, way, way, g).start()

    def gathered(row, half, g):
        total = terms[g, OWN, row, half].astype(jnp.float32)
        for way in range(2):
            if row == 1 or way == half:
                near(row, way, half, g).wait_recv()
                total = total + near_in[g, way, row, half].astype(jnp.float32)
        return total

    groups, ways = range(GROUPS), range(2)
    for g in groups:
        product(FAR, 2, g)
        for way in ways:
            far(0, way, g).start()
    for way in ways:
        for g in groups:
            product(RIGHT + way, 1 - 2 * way, g)
            relay(way, g).start()
    for g in groups:
        for way in ways:
            carry(0, way, g)
    for g in groups:
        for way in ways:
            far(1, way, g).start()
    for g in groups:
        product(OWN, 0, g)
    for g in groups:
        for way in ways:
            take(way, g)
    for g in groups:
        for half in range(HALVES):
            pair_out[g, half] = gathered(0, half, g).astype(jnp.bfloat16)
            across(half, g).start()
    for g in groups:
        for way in ways:
            carry(1, way, g)
    for g in groups:
        for half in range(HALVES):
            total = gathered(1, half, g)
            across(half, g).wait_recv()
            total = total + pair_in[g, half].astype(jnp.float32)
            first = (g * HALVES + half) * width
            out_ref[:, first : first + width] = total.astype(jnp.bfloat16)
    for g in groups:
        for way in ways:
            for row in range(2):
                far(row, way, g).wait_send()
                for half in range(HALVES):
                    if row == 1 or way == half:
                        near(row, way, half, g).wait_send()
            relay(way, g).wait_send()
        for half in range(HALVES):
            across(half, g).wait_send()


def reduce_out(mixed, w_output, groups):
    rows, width = mixed.shape[0], w_output.shape[1]
    shard, half = rows // groups, width // (GROUPS * HALVES)
    vmem = pl.BlockSpec(memory_space=pltpu.VMEM)
    dma = pltpu.SemaphoreType.DMA
    piece = (shard, half)
    return pl.pallas_call(
        functools.partial(reduce_kernel, shard),
        in_specs=[vmem, vmem],
        out_specs=vmem,
        out_shape=jax.ShapeDtypeStruct((shard, width), jnp.bfloat16),
        scratch_shapes=[
            pltpu.VMEM((GROUPS, 4, 2, HALVES, *piece), jnp.bfloat16),
            pltpu.VMEM((GROUPS, 2, 2, *piece), jnp.bfloat16),
            pltpu.VMEM((GROUPS, 2, 2, HALVES, *piece), jnp.bfloat16),
            pltpu.VMEM((GROUPS, HALVES, *piece), jnp.bfloat16),
            pltpu.VMEM((GROUPS, HALVES, *piece), jnp.bfloat16),
            pltpu.VMEM((GROUPS, 2, *piece), jnp.bfloat16),
            dma((GROUPS, 2, 2)), dma((GROUPS, 2, 2)),
            dma((GROUPS, 2, 2, HALVES)), dma((GROUPS, 2, 2, HALVES)),
            dma((GROUPS, HALVES)), dma((GROUPS, HALVES)),
            dma((GROUPS, 2)), dma((GROUPS, 2)),
        ],
        compiler_params=pltpu.CompilerParams(collective_id=1, has_side_effects=True),
    )(mixed, w_output)


Z_RING = 8
RELAY = False
SPLIT = (0, 3, 4, 5, 7)
ORDER = (
    (2, 0, 0, 0), (4, 0, 0, 0), (5, 0, 0, 0), (4, 0, 1, 0), (4, 0, 1, 1), (0, 0, 0, 0),
    (0, 0, 1, 0), (1, 0, 0, 0), (4, 0, 2, 0), (4, 0, 2, 1), (5, 0, 1, 0), (5, 0, 1, 1),
    (4, 0, 3, 0), (2, 1, 0, 0), (1, 1, 0, 0), (2, 2, 0, 0), (2, 4, 0, 0), (4, 4, 0, 0),
    (2, 3, 0, 0), (4, 3, 0, 0), (4, 2, 0, 0), (4, 1, 0, 0), (4, 0, 3, 1), (4, 0, 4, 0),
    (5, 0, 2, 0), (5, 0, 2, 1), (5, 0, 3, 0), (4, 4, 1, 0), (4, 4, 1, 1), (5, 4, 0, 0),
    (3, 0, 0, 0), (0, 1, 0, 0), (4, 3, 1, 0), (4, 3, 1, 1), (5, 0, 3, 1), (5, 3, 0, 0),
    (3, 0, 1, 0), (4, 2, 1, 0), (4, 2, 1, 1), (4, 1, 1, 0), (4, 1, 1, 1), (4, 4, 2, 0),
    (4, 4, 2, 1), (5, 0, 4, 0), (4, 3, 2, 0), (4, 3, 2, 1), (5, 3, 1, 0), (0, 1, 1, 0),
    (2, 5, 0, 0), (2, 6, 0, 0), (4, 5, 0, 0), (4, 2, 2, 0), (4, 2, 2, 1), (4, 1, 2, 0),
    (4, 4, 3, 0), (4, 4, 3, 1), (4, 1, 2, 1), (4, 3, 3, 0), (4, 3, 3, 1), (5, 3, 1, 1),
    (5, 3, 2, 0), (5, 3, 2, 1), (5, 4, 1, 0), (5, 4, 1, 1), (5, 4, 2, 0), (5, 4, 2, 1),
    (5, 5, 0, 0), (4, 6, 0, 0), (4, 5, 1, 0), (4, 5, 1, 1), (5, 4, 3, 0), (2, 7, 0, 0),
    (4, 7, 0, 0), (4, 2, 3, 0), (4, 2, 3, 1), (4, 1, 3, 0), (4, 4, 4, 0), (4, 3, 4, 1),
    (4, 1, 3, 1), (5, 3, 3, 0), (5, 3, 3, 1), (5, 4, 3, 1), (5, 5, 1, 0), (3, 1, 0, 0),
    (4, 6, 1, 0), (4, 7, 1, 0), (4, 7, 1, 1), (4, 6, 1, 1), (4, 5, 2, 0), (4, 5, 2, 1),
    (4, 2, 4, 0), (4, 2, 4, 1), (4, 1, 4, 0), (4, 1, 4, 1), (5, 3, 4, 1), (5, 4, 4, 0),
    (5, 5, 1, 1), (5, 7, 0, 0), (3, 1, 1, 0), (4, 7, 2, 1), (4, 6, 2, 0), (5, 7, 1, 0),
    (5, 7, 1, 1), (4, 7, 2, 0), (5, 5, 2, 0), (4, 6, 2, 1), (4, 5, 3, 0), (5, 5, 2, 1),
    (4, 5, 3, 1), (4, 7, 3, 1), (5, 7, 2, 1), (4, 6, 3, 0), (5, 7, 2, 0), (4, 7, 3, 0),
    (5, 5, 3, 0), (4, 6, 3, 1), (5, 5, 3, 1), (4, 5, 4, 1), (4, 7, 4, 1), (5, 7, 3, 1),
    (4, 6, 4, 0), (5, 7, 3, 0), (4, 6, 4, 1), (5, 5, 4, 1), (5, 7, 4, 1),
)


def gather_kernel(
    tokens_ref, wq_ref, wk_ref, wv_ref, pos_ref, inv_ref, q_ref, kv_ref,
    cos_ref, sin_ref, tok, wq, wkv, mine,
    load_sem, own_send, own_recv, far_send, far_recv,
    mine_sem, y_send, y_recv, z_send, z_recv, fwd_send, fwd_recv, core_send, core_recv,
):
    at = places()
    side = ({"grp": at(1, False)}, {"grp": at(-1, False)})
    pair = {"grp": at(0, True)}
    blk = lax.axis_index("blk")
    core, near_y, depth = lax.rem(blk, 2), lax.rem(blk // 2, 2), blk // 4
    shard, half = tokens_ref.shape[0], tokens_ref.shape[0] // 2

    def deep(step):
        return lax.rem(depth + step + Z_RING, Z_RING)

    z_side = tuple({"blk": (deep(d) * 2 + near_y) * 2 + core} for d in (1, -1))
    y_side = {"blk": (depth * 2 + 1 - near_y) * 2 + core}
    core_side = {"blk": (depth * 2 + near_y) * 2 + 1 - core}

    loads = [
        pltpu.make_async_copy(tokens_ref, tok.at[0, 0], load_sem.at[0]),
        pltpu.make_async_copy(wk_ref, wkv.at[:, pl.ds(0, HEAD)], load_sem.at[1]),
        pltpu.make_async_copy(wv_ref, wkv.at[:, pl.ds(HEAD, HEAD)], load_sem.at[2]),
        pltpu.make_async_copy(wq_ref, wq, load_sem.at[3]),
    ]
    for load in loads:
        load.start()
    greet([*side, pair, *z_side, y_side, core_side])

    def rows(row, place, h):
        return tok.at[row, place, pl.ds(h * half, half)]

    def hand(row, way, h):
        return pltpu.make_async_remote_copy(
            rows(row, 0, h), rows(row, 1 + way, h),
            own_send.at[row, way, h], own_recv.at[row, way, h],
            device_id=side[way], device_id_type=MESH_ID,
        )

    def cross(h):
        return pltpu.make_async_remote_copy(
            rows(0, 0, h), rows(1, 0, h), own_send.at[0, 2, h], own_recv.at[0, 2, h],
            device_id=pair, device_id_type=MESH_ID,
        )

    def further(row, way):
        return pltpu.make_async_remote_copy(
            rows(row, 1 + way, way), rows(row, 3, way),
            far_send.at[row, way], far_recv.at[row, way],
            device_id=side[way], device_id_type=MESH_ID,
        )

    def relay(way):
        return pltpu.make_async_remote_copy(
            rows(0, 1 + way, way), rows(1, 1 + way, way),
            own_send.at[1, way, way], own_recv.at[1, way, way],
            device_id=pair, device_id_type=MESH_ID,
        )

    def pass_on(row, way):
        hand(row, way, way).wait_recv()
        further(row, way).start()
        if RELAY and row == 0:
            relay(way).start()

    def cross_on(h):
        cross(h).wait_recv()
        for way in range(2):
            if not (RELAY and way == h):
                hand(1, way, h).start()

    order = ((0, 0, 0), (0, 1, -1), (0, 2, 1), (0, 3, 2), (1, 0, 0), (1, 1, -1), (1, 2, 1), (1, 3, 2))

    def spot(u):
        row, _, dc = order[u]
        return at(dc, row == 1)

    def tables(u):
        here = pl.ds(pl.multiple_of(spot(u) * shard, shard), shard)
        return cos_ref[here, :], sin_ref[here, :]

    def keep(u):
        return pltpu.make_async_copy(
            mine.at[u], kv_ref.at[core, depth, spot(u), near_y], mine_sem.at[u]
        )

    def y_copy(u):
        return pltpu.make_async_remote_copy(
            mine.at[u], kv_ref.at[core, depth, spot(u), near_y],
            y_send.at[u], y_recv.at[u],
            device_id=y_side, device_id_type=MESH_ID,
        )

    def z_copy(u, way, hop, own=True):
        origin = deep(-hop if way == 0 else hop)
        ref = kv_ref.at[core, origin, spot(u)]
        if u in SPLIT:
            ref = kv_ref.at[core, origin, spot(u), near_y]
        elif hop == 3:
            ref = kv_ref.at[core, origin, spot(u), way]
        source = mine.at[u] if u in SPLIT and hop == 0 and own else ref
        return pltpu.make_async_remote_copy(
            source, ref, z_send.at[way, hop, u], z_recv.at[way, hop, u],
            device_id=z_side[way], device_id_type=MESH_ID,
        )

    def z_arrival(u, way, hop):
        origin = deep(-hop - 1 if way == 0 else hop + 1)
        ref = kv_ref.at[core, origin, spot(u)]
        if u in SPLIT:
            ref = kv_ref.at[core, origin, spot(u), near_y]
        elif hop == 3:
            ref = kv_ref.at[core, origin, spot(u), way]
        return pltpu.make_async_remote_copy(
            ref, ref, z_send.at[way, hop, u], z_recv.at[way, hop, u],
            device_id=z_side[way], device_id_type=MESH_ID,
        )

    def core_copy(u, origin, y=None, source=None):
        ref = kv_ref.at[core, origin, spot(u)]
        if y is not None:
            ref = kv_ref.at[core, origin, spot(u), y]
        return pltpu.make_async_remote_copy(
            ref if source is None else source, ref, core_send, core_recv,
            device_id=core_side, device_id_type=MESH_ID,
        )

    def origin_of(stage, way):
        return deep(-stage if way == 0 else stage)

    def y_forward(u, stage, way):
        ref = kv_ref.at[core, origin_of(stage, way), spot(u), near_y]
        return pltpu.make_async_remote_copy(
            ref, ref, fwd_send.at[u, way, stage - 1], fwd_recv.at[u, way, stage - 1],
            device_id=y_side, device_id_type=MESH_ID,
        )

    def y_landed(u, stage, way):
        ref = kv_ref.at[core, origin_of(stage, way), spot(u), 1 - near_y]
        return pltpu.make_async_remote_copy(
            ref, ref, fwd_send.at[u, way, stage - 1], fwd_recv.at[u, way, stage - 1],
            device_id=y_side, device_id_type=MESH_ID,
        )

    def hops(u, stage, way):
        return stage < 3 or (stage == 3 and (u not in SPLIT or way == u % 2))

    def keys(u):
        row, place, _ = order[u]
        y = jnp.dot(tok[row, place], wkv[...], preferred_element_type=jnp.float32)
        cosine, sine = tables(u)
        mine[u, :, :HEAD] = turn(y[:, :HEAD], cosine, sine).astype(jnp.bfloat16)
        mine[u, :, HEAD:] = y[:, HEAD:].astype(jnp.bfloat16)
        keep(u).start()
        y_copy(u).start()

    def ring(u, stage, way):
        if stage == 0:
            if u not in SPLIT:
                keep(u).wait()
                y_copy(u).wait_recv()
            z_copy(u, 0, 0).start()
            z_copy(u, 1, 0).start()
            if u in SPLIT:
                core_copy(u, depth, near_y, mine.at[u]).start()
            else:
                core_copy(u, depth).start()
            return
        z_arrival(u, way, stage - 1).wait_recv()
        if hops(u, stage, way):
            z_copy(u, way, stage, False).start()
        origin = origin_of(stage, way)
        if u in SPLIT:
            y_forward(u, stage, way).start()
            core_copy(u, origin, near_y).start()
        elif stage < 4:
            core_copy(u, origin).start()
        else:
            core_copy(u, origin, way).start()

    def landed(u, stage, way):
        if stage == 0:
            y_copy(u).wait_recv()
            core_copy(u, depth, 1 - near_y).start()
        else:
            y_landed(u, stage, way).wait_recv()
            core_copy(u, origin_of(stage, way), 1 - near_y).start()

    def queries(row, part):
        wide = 2 * HEAD
        x = tok[row].reshape(4 * shard, tok.shape[-1])
        cols = slice(part * wide, (part + 1) * wide)
        y = jnp.dot(x, wq[:, cols], preferred_element_type=jnp.float32)
        for n in range(4):
            u = next(i for i, o in enumerate(order) if o[:2] == (row, n))
            cosine, sine = tables(u)
            here = pl.ds(pl.multiple_of(spot(u) * shard, shard), shard)
            for h in range(2):
                v = y[n * shard : (n + 1) * shard, h * HEAD : (h + 1) * HEAD]
                q_ref[here, part * wide + h * HEAD : part * wide + (h + 1) * HEAD] = turn(
                    v, cosine, sine
                ).astype(jnp.bfloat16)

    def project_keys(u):
        row, place, _ = order[u]
        if u == 0:
            loads[1].wait()
            loads[2].wait()
        elif place == 3:
            further(row, 0).wait_recv()
            further(row, 1).wait_recv()
        elif place:
            hand(row, place - 1, 2 - place).wait_recv()
        keys(u)

    def project_queries(row, part):
        if (row, part) == (0, 0):
            loads[3].wait()
        queries(row, part)

    loads[0].wait()
    for h in range(2):
        hand(0, 0, h).start()
        hand(0, 1, 1 - h).start()
    for h in range(2):
        cross(h).start()
    lanes = lax.broadcasted_iota(jnp.int32, (1, HEAD), 1)
    flip = jnp.where(lanes < HEAD // 2, -1.0, 1.0)

    @pl.loop(0, pos_ref.shape[0])
    def _(step):
        here = pl.ds(pl.multiple_of(step * HEAD, HEAD), HEAD)
        spread = jnp.broadcast_to(pos_ref[pl.ds(step, 1), :].astype(jnp.float32), (HEAD, HEAD))
        angles = spread.T * inv_ref[...]
        cos_ref[here, :] = jnp.cos(angles)
        sin_ref[here, :] = jnp.sin(angles) * flip

    for kind, *rest in ORDER:
        if kind == 0:
            pass_on(*rest[:2])
        elif kind == 1:
            cross_on(rest[0])
        elif kind == 2:
            project_keys(rest[0])
        elif kind == 3:
            project_queries(*rest[:2])
        elif kind == 4:
            ring(*rest)
        else:
            landed(*rest)

    for h in range(2):
        cross(h).wait_send()
        for row in range(2):
            for way in range(2):
                hand(row, way, h).wait_send()
    for row in range(2):
        for way in range(2):
            further(row, way).wait_send()
    for u in range(len(order)):
        y_copy(u).wait_send()
        if u in SPLIT:
            keep(u).wait()
        for way in range(2):
            for stage in range(4):
                if hops(u, stage, way):
                    z_copy(u, way, stage).wait_send()
            if u in SPLIT:
                for stage in range(1, 5):
                    if hops(u, stage - 1, way):
                        y_forward(u, stage, way).wait_send()
    done = kv_ref.at[core]
    pltpu.make_async_copy(done, done, core_send).wait()
    done = kv_ref.at[1 - core]
    pltpu.make_async_copy(done, done, core_recv).wait()


def gather(tokens, wq, wk, wv, positions, groups):
    shard, width = tokens.shape
    units = groups
    hbm, vmem = pl.BlockSpec(memory_space=pl.ANY), pl.BlockSpec(memory_space=pltpu.VMEM)
    dma = pltpu.SemaphoreType.DMA
    return pl.pallas_call(
        gather_kernel,
        in_specs=[hbm, hbm, hbm, hbm, vmem, vmem],
        out_specs=[vmem, hbm],
        out_shape=[
            jax.ShapeDtypeStruct((shard * groups, wq.shape[1]), jnp.bfloat16),
            jax.ShapeDtypeStruct((2, Z_RING, groups, 2, shard, 2 * HEAD), jnp.bfloat16),
        ],
        scratch_shapes=[
            pltpu.VMEM((shard * groups, HEAD), jnp.float32),
            pltpu.VMEM((shard * groups, HEAD), jnp.float32),
            pltpu.VMEM((2, RING, shard, width), jnp.bfloat16),
            pltpu.VMEM(wq.shape, jnp.bfloat16),
            pltpu.VMEM((width, 2 * HEAD), jnp.bfloat16),
            pltpu.VMEM((units, shard, 2 * HEAD), jnp.bfloat16),
            dma((4,)),
            dma((2, 3, 2)), dma((2, 3, 2)), dma((2, 2)), dma((2, 2)),
            dma((units,)), dma((units,)), dma((units,)),
            dma((2, 4, units)), dma((2, 4, units)),
            dma((units, 2, 4)), dma((units, 2, 4)),
            dma, dma,
        ],
        compiler_params=pltpu.CompilerParams(collective_id=0, has_side_effects=True),
    )(tokens, wq, wk, wv, positions.reshape(-1, HEAD), inverse_lanes())


def body(tokens, w_query, key_weight, value_weight, w_output, block_mask, positions):
    groups = lax.axis_size("grp")
    q, kv = gather(tokens, w_query, key_weight, value_weight, positions, groups)
    mixed = attend(block_mask, q, kv)
    return reduce_out(mixed, w_output, groups)


def solution(mesh):
    return jax.shard_map(
        body,
        mesh=mesh,
        in_specs=(
            P(("blk", "grp"), None),
            P(None, "grp"),
            P(None, "grp"),
            P(None, "grp"),
            P("grp", None),
            P("blk", None),
            P("blk"),
        ),
        out_specs=P(("blk", "grp"), None),
        check_vma=False,
    )
```

```python
import functools

import jax
import jax.numpy as jnp
import numpy as np
from jax import lax
from jax.experimental import pallas as pl
from jax.experimental.pallas import tpu as pltpu
from jax.sharding import PartitionSpec as P

HEAD = 128
BLOCK = 128
NEG = -1e30
LOG2E = 1.4426950408889634
SCALE2 = HEAD ** (-0.5) * LOG2E


def inverse_lanes():
    half = HEAD // 2
    inverse = np.power(
        np.float32(500000.0), -(np.float32(2.0) * np.arange(half, dtype=np.float32)) / np.float32(HEAD)
    ).astype(np.float32)
    return jnp.asarray(np.concatenate([inverse, inverse])[None, :])


def turn(v, cosine, sine):
    return v * cosine + pltpu.roll(v, HEAD // 2, 1) * sine


def score(q, k):
    return lax.dot_general(q, k, (((1,), (1,)), ((), ())), preferred_element_type=jnp.float32)


def attend_kernel(
    n_blocks, heads, mask_ref, q_ref, kv_ref, out_ref, near, stream, ahead, sem, stream_sem
):
    blk = lax.axis_index("blk")
    rows = q_ref.shape[0] // BLOCK
    shard = kv_ref.shape[4]
    pieces = BLOCK // shard
    lanes = lax.broadcasted_iota(jnp.int32, (1, n_blocks), 1)
    for r in range(rows):
        i = blk * rows + r
        live = mask_ref[r : r + 1, :] != 0
        fixed = (jnp.abs(lanes - i) <= 1) | (lanes < 1)
        left = jnp.where(live & jnp.logical_not(fixed), lanes, n_blocks)
        ids = [0, jnp.maximum(i - 1, 0), i, jnp.minimum(i + 1, n_blocks - 1)]
        last = jnp.int32(-1)
        for _ in range(3):
            last = jnp.min(jnp.where(left > last, left, n_blocks))
            ids.append(jnp.minimum(last, n_blocks - 1))
        for s, j in enumerate(ids):
            owner = j // rows
            for h in range(pieces):
                pltpu.make_async_copy(
                    kv_ref.at[
                        lax.rem(owner, 2),
                        owner // 4,
                        lax.rem(j, rows) * pieces + h,
                        lax.rem(owner // 2, 2),
                    ],
                    near.at[r, pl.ds(s * BLOCK + h * shard, shard)],
                    sem.at[r],
                ).start()

    def queries(r):
        return jnp.concatenate(
            [
                q_ref[r * BLOCK : (r + 1) * BLOCK, h * HEAD : (h + 1) * HEAD]
                for h in range(heads)
            ],
            axis=0,
        )

    def put(r, mixed):
        for h in range(heads):
            out_ref[r * BLOCK : (r + 1) * BLOCK, h * HEAD : (h + 1) * HEAD] = mixed[
                h * BLOCK : (h + 1) * BLOCK
            ].astype(jnp.bfloat16)

    def near_row(r):
        i = blk * rows + r
        s = score(queries(r), near[r, :, :HEAD])
        parts = [
            jnp.where(i == 1, NEG, s[:, :BLOCK]),
            s[:, BLOCK : 3 * BLOCK],
            jnp.where(i == n_blocks - 1, NEG, s[:, 3 * BLOCK : 4 * BLOCK]),
            s[:, 4 * BLOCK :],
        ]
        s = jnp.concatenate(parts, axis=1)
        top = jnp.max(s, axis=1, keepdims=True)
        p = jnp.exp2(s * SCALE2 - top * SCALE2)
        total = jnp.sum(p, axis=1, keepdims=True)
        mixed = jnp.dot(
            p.astype(jnp.bfloat16), near[r, :, HEAD:], preferred_element_type=jnp.float32
        )
        put(r, mixed / total)

    for r in range(rows):
        pltpu.make_async_copy(near.at[r], near.at[r], sem.at[r]).wait()
        if r:
            near_row(r)

    @pl.when(blk != 0)
    def _():
        near_row(0)

    @pl.when(blk == 0)
    def _():
        steps = kv_ref.shape[0] * kv_ref.shape[1]

        def fetch(step, slot):
            return pltpu.make_async_copy(
                kv_ref.at[step // kv_ref.shape[1], lax.rem(step, kv_ref.shape[1])],
                stream.at[slot],
                stream_sem.at[slot],
            )

        q = queries(0)
        n = q.shape[0]
        for step in range(steps):
            fetch(step, step).start()

        def keys_of(step):
            return stream[step].reshape(-1, 2 * HEAD)

        def fold(s, both, state):
            top, total, accum = state
            new = jnp.maximum(top, jnp.max(s, axis=1, keepdims=True))
            p = jnp.exp2(s * SCALE2 - new * SCALE2)
            factor = jnp.exp2((top - new) * SCALE2)
            total = total * factor + jnp.sum(p, axis=1, keepdims=True)
            accum = accum * factor + jnp.dot(
                p.astype(jnp.bfloat16), both[:, HEAD:], preferred_element_type=jnp.float32
            )
            return new, total, accum

        fetch(0, 0).wait()
        ahead[0] = score(q, keys_of(0)[:, :HEAD])

        def body(pair, state):
            first = pair * 2
            after = jnp.minimum(first + 2, steps - 1)
            fetch(first + 1, first + 1).wait()

            @pl.when(first + 2 < steps)
            def _():
                fetch(after, after).wait()

            ahead[1] = score(q, keys_of(first + 1)[:, :HEAD])
            state = fold(ahead[0], keys_of(first), state)
            ahead[0] = score(q, keys_of(after)[:, :HEAD])
            return fold(ahead[1], keys_of(first + 1), state)

        top, total, accum = lax.fori_loop(
            0,
            steps // 2,
            body,
            (
                jnp.full((n, 1), NEG, jnp.float32),
                jnp.zeros((n, 1), jnp.float32),
                jnp.zeros((n, HEAD), jnp.float32),
            ),
        )
        put(0, accum / total)


def attend(block_mask, q, kv):
    rows = q.shape[0] // BLOCK
    n_blocks = block_mask.shape[1]
    heads = q.shape[1] // HEAD
    vmem = pl.BlockSpec(memory_space=pltpu.VMEM)
    return pl.pallas_call(
        functools.partial(attend_kernel, n_blocks, heads),
        in_specs=[vmem, vmem, pl.BlockSpec(memory_space=pl.ANY)],
        out_specs=vmem,
        out_shape=jax.ShapeDtypeStruct(q.shape, jnp.bfloat16),
        scratch_shapes=[
            pltpu.VMEM((rows, 7 * BLOCK, 2 * HEAD), jnp.bfloat16),
            pltpu.VMEM((16, *kv.shape[2:]), jnp.bfloat16),
            pltpu.VMEM((2, heads * BLOCK, 1024), jnp.float32),
            pltpu.SemaphoreType.DMA((rows,)),
            pltpu.SemaphoreType.DMA((16,)),
        ],
    )(block_mask, q, kv)


MESH_ID = pl.DeviceIdType.MESH
RING = 4
HALVES = 2


def places():
    g = lax.axis_index("grp")
    col, row = lax.rem(g, RING), g // RING

    def at(dc, flip):
        r = 1 - row if flip else row
        return r * RING + lax.rem(col + dc + RING, RING)

    return at


def greet(peers):
    barrier = pltpu.get_barrier_semaphore()
    for peer in peers:
        pl.semaphore_signal(barrier, inc=1, device_id=peer, device_id_type=MESH_ID)
    pl.semaphore_wait(barrier, len(peers))


GROUPS = 2


def reduce_kernel(
    shard, mixed_ref, w_ref, out_ref,
    terms, far_in, near_in, pair_out, pair_in, relay_in,
    far_send, far_recv, near_send, near_recv, pair_send, pair_recv, relay_send, relay_recv,
):
    at = places()
    right, left, pair = at(1, False), at(-1, False), at(0, True)
    side = ({"grp": right}, {"grp": left})
    width = w_ref.shape[1] // (GROUPS * HALVES)
    FAR, RIGHT, LEFT, OWN = 0, 1, 2, 3
    greet([side[0], side[1], {"grp": pair}])

    def product(slot, dcs, g):
        lhs = jnp.concatenate(
            [
                mixed_ref[pl.ds(pl.multiple_of(at(dc, flip) * shard, shard), shard), :]
                for dc in dcs
                for flip in (True, False)
            ],
            axis=0,
        )
        step = 256
        for half in range(HALVES):
            for c in range(width // step):
                cols = slice(c * step, (c + 1) * step)
                first = (g * HALVES + half) * width + c * step
                t = jnp.dot(
                    lhs, w_ref[:, first : first + step], preferred_element_type=jnp.float32
                )
                for n in range(2 * len(dcs)):
                    terms[g, slot + n // 2, n % 2, half, :, cols] = t[
                        n * shard : (n + 1) * shard
                    ].astype(jnp.bfloat16)

    def far(row, way, g):
        return pltpu.make_async_remote_copy(
            terms.at[g, FAR, row, way], far_in.at[g, way, row],
            far_send.at[g, way, row], far_recv.at[g, way, row],
            device_id=side[way], device_id_type=MESH_ID,
        )

    def near(row, way, half, g):
        return pltpu.make_async_remote_copy(
            terms.at[g, RIGHT + way, row, half], near_in.at[g, way, row, half],
            near_send.at[g, way, row, half], near_recv.at[g, way, row, half],
            device_id=side[way], device_id_type=MESH_ID,
        )

    def across(half, g):
        return pltpu.make_async_remote_copy(
            pair_out.at[g, half], pair_in.at[g, half],
            pair_send.at[g, half], pair_recv.at[g, half],
            device_id={"grp": pair}, device_id_type=MESH_ID,
        )

    def relay(way, g):
        return pltpu.make_async_remote_copy(
            terms.at[g, RIGHT + way, 0, 1 - way], relay_in.at[g, way],
            relay_send.at[g, way], relay_recv.at[g, way],
            device_id={"grp": pair}, device_id_type=MESH_ID,
        )

    def join(slot, row, half, g, more):
        terms[g, slot, row, half] = (
            terms[g, slot, row, half].astype(jnp.float32) + more.astype(jnp.float32)
        ).astype(jnp.bfloat16)

    def take(way, g):
        relay(way, g).wait_recv()
        join(RIGHT + way, 1, 1 - way, g, relay_in[g, way])
        near(1, way, 1 - way, g).start()

    def carry(row, way, g):
        far(row, way, g).wait_recv()
        join(RIGHT + way, row, way, g, far_in[g, way, row])
        near(row, way, way, g).start()

    def gathered(row, half, g):
        total = terms[g, OWN, row, half].astype(jnp.float32)
        for way in range(2):
            if row == 1 or way == half:
                near(row, way, half, g).wait_recv()
                total = total + near_in[g, way, row, half].astype(jnp.float32)
        return total

    groups, ways = range(GROUPS), range(2)
    for g in groups:
        product(FAR, (2,), g)
        for way in ways:
            far(0, way, g).start()
    for g in groups:
        product(RIGHT, (1, -1, 0), g)
        for way in ways:
            relay(way, g).start()
    for g in groups:
        for way in ways:
            carry(0, way, g)
    for g in groups:
        for way in ways:
            far(1, way, g).start()
    for g in groups:
        for way in ways:
            take(way, g)
    for g in groups:
        for half in range(HALVES):
            pair_out[g, half] = gathered(0, half, g).astype(jnp.bfloat16)
            across(half, g).start()
    for g in groups:
        for way in ways:
            carry(1, way, g)
    for g in groups:
        for half in range(HALVES):
            total = gathered(1, half, g)
            across(half, g).wait_recv()
            total = total + pair_in[g, half].astype(jnp.float32)
            first = (g * HALVES + half) * width
            out_ref[:, first : first + width] = total.astype(jnp.bfloat16)
    for g in groups:
        for way in ways:
            for row in range(2):
                far(row, way, g).wait_send()
                for half in range(HALVES):
                    if row == 1 or way == half:
                        near(row, way, half, g).wait_send()
            relay(way, g).wait_send()
        for half in range(HALVES):
            across(half, g).wait_send()


def reduce_out(mixed, w_output, groups):
    rows, width = mixed.shape[0], w_output.shape[1]
    shard, half = rows // groups, width // (GROUPS * HALVES)
    vmem = pl.BlockSpec(memory_space=pltpu.VMEM)
    dma = pltpu.SemaphoreType.DMA
    piece = (shard, half)
    return pl.pallas_call(
        functools.partial(reduce_kernel, shard),
        in_specs=[vmem, vmem],
        out_specs=vmem,
        out_shape=jax.ShapeDtypeStruct((shard, width), jnp.bfloat16),
        scratch_shapes=[
            pltpu.VMEM((GROUPS, 4, 2, HALVES, *piece), jnp.bfloat16),
            pltpu.VMEM((GROUPS, 2, 2, *piece), jnp.bfloat16),
            pltpu.VMEM((GROUPS, 2, 2, HALVES, *piece), jnp.bfloat16),
            pltpu.VMEM((GROUPS, HALVES, *piece), jnp.bfloat16),
            pltpu.VMEM((GROUPS, HALVES, *piece), jnp.bfloat16),
            pltpu.VMEM((GROUPS, 2, *piece), jnp.bfloat16),
            dma((GROUPS, 2, 2)), dma((GROUPS, 2, 2)),
            dma((GROUPS, 2, 2, HALVES)), dma((GROUPS, 2, 2, HALVES)),
            dma((GROUPS, HALVES)), dma((GROUPS, HALVES)),
            dma((GROUPS, 2)), dma((GROUPS, 2)),
        ],
        compiler_params=pltpu.CompilerParams(collective_id=1, has_side_effects=True),
    )(mixed, w_output)


Z_RING = 8
RELAY = False
SPLIT = (0, 3, 4, 5, 7)
ORDER = (
    (2, 0, 0, 0), (4, 0, 0, 0), (5, 0, 0, 0), (4, 0, 1, 0), (4, 0, 1, 1), (0, 0, 0, 0),
    (0, 0, 1, 0), (1, 0, 0, 0), (4, 0, 2, 0), (4, 0, 2, 1), (5, 0, 1, 0), (5, 0, 1, 1),
    (4, 0, 3, 0), (2, 1, 0, 0), (1, 1, 0, 0), (2, 2, 0, 0), (2, 4, 0, 0), (4, 4, 0, 0),
    (2, 3, 0, 0), (4, 3, 0, 0), (4, 2, 0, 0), (4, 1, 0, 0), (4, 0, 3, 1), (4, 0, 4, 0),
    (5, 0, 2, 0), (5, 0, 2, 1), (5, 0, 3, 0), (4, 4, 1, 0), (4, 4, 1, 1), (5, 4, 0, 0),
    (3, 0, 0, 0), (0, 1, 0, 0), (4, 3, 1, 0), (4, 3, 1, 1), (5, 0, 3, 1), (5, 3, 0, 0),
    (3, 0, 1, 0), (4, 2, 1, 0), (4, 2, 1, 1), (4, 1, 1, 0), (4, 1, 1, 1), (4, 4, 2, 0),
    (4, 4, 2, 1), (5, 0, 4, 0), (4, 3, 2, 0), (4, 3, 2, 1), (5, 3, 1, 0), (0, 1, 1, 0),
    (2, 5, 0, 0), (2, 6, 0, 0), (4, 5, 0, 0), (4, 2, 2, 0), (4, 2, 2, 1), (4, 1, 2, 0),
    (4, 4, 3, 0), (4, 4, 3, 1), (4, 1, 2, 1), (4, 3, 3, 0), (4, 3, 3, 1), (5, 3, 1, 1),
    (5, 3, 2, 0), (5, 3, 2, 1), (5, 4, 1, 0), (5, 4, 1, 1), (5, 4, 2, 0), (5, 4, 2, 1),
    (5, 5, 0, 0), (4, 6, 0, 0), (4, 5, 1, 0), (4, 5, 1, 1), (5, 4, 3, 0), (2, 7, 0, 0),
    (4, 7, 0, 0), (4, 2, 3, 0), (4, 2, 3, 1), (4, 1, 3, 0), (4, 4, 4, 0), (4, 3, 4, 1),
    (4, 1, 3, 1), (5, 3, 3, 0), (5, 3, 3, 1), (5, 4, 3, 1), (5, 5, 1, 0), (3, 1, 0, 0),
    (4, 6, 1, 0), (4, 7, 1, 0), (4, 7, 1, 1), (4, 6, 1, 1), (4, 5, 2, 0), (4, 5, 2, 1),
    (4, 2, 4, 0), (4, 2, 4, 1), (4, 1, 4, 0), (4, 1, 4, 1), (5, 3, 4, 1), (5, 4, 4, 0),
    (5, 5, 1, 1), (5, 7, 0, 0), (3, 1, 1, 0), (4, 7, 2, 1), (4, 6, 2, 0), (5, 7, 1, 0),
    (5, 7, 1, 1), (4, 7, 2, 0), (5, 5, 2, 0), (4, 6, 2, 1), (4, 5, 3, 0), (5, 5, 2, 1),
    (4, 5, 3, 1), (4, 7, 3, 1), (5, 7, 2, 1), (4, 6, 3, 0), (5, 7, 2, 0), (4, 7, 3, 0),
    (5, 5, 3, 0), (4, 6, 3, 1), (5, 5, 3, 1), (4, 5, 4, 1), (4, 7, 4, 1), (5, 7, 3, 1),
    (4, 6, 4, 0), (5, 7, 3, 0), (4, 6, 4, 1), (5, 5, 4, 1), (5, 7, 4, 1),
)


def gather_kernel(
    tokens_ref, wq_ref, wk_ref, wv_ref, pos_ref, inv_ref, q_ref, kv_ref,
    cos_ref, sin_ref, tok, wq, wkv, mine,
    load_sem, own_send, own_recv, far_send, far_recv,
    mine_sem, y_send, y_recv, z_send, z_recv, fwd_send, fwd_recv, core_send, core_recv,
):
    at = places()
    side = ({"grp": at(1, False)}, {"grp": at(-1, False)})
    pair = {"grp": at(0, True)}
    blk = lax.axis_index("blk")
    core, near_y, depth = lax.rem(blk, 2), lax.rem(blk // 2, 2), blk // 4
    shard, half = tokens_ref.shape[0], tokens_ref.shape[0] // 2

    def deep(step):
        return lax.rem(depth + step + Z_RING, Z_RING)

    z_side = tuple({"blk": (deep(d) * 2 + near_y) * 2 + core} for d in (1, -1))
    y_side = {"blk": (depth * 2 + 1 - near_y) * 2 + core}
    core_side = {"blk": (depth * 2 + near_y) * 2 + 1 - core}

    loads = [
        pltpu.make_async_copy(tokens_ref, tok.at[0, 0], load_sem.at[0]),
        pltpu.make_async_copy(wk_ref, wkv.at[:, pl.ds(0, HEAD)], load_sem.at[1]),
        pltpu.make_async_copy(wv_ref, wkv.at[:, pl.ds(HEAD, HEAD)], load_sem.at[2]),
        pltpu.make_async_copy(wq_ref, wq, load_sem.at[3]),
    ]
    for load in loads:
        load.start()
    greet([*side, pair, *z_side, y_side, core_side])

    def rows(row, place, h):
        return tok.at[row, place, pl.ds(h * half, half)]

    def hand(row, way, h):
        return pltpu.make_async_remote_copy(
            rows(row, 0, h), rows(row, 1 + way, h),
            own_send.at[row, way, h], own_recv.at[row, way, h],
            device_id=side[way], device_id_type=MESH_ID,
        )

    def cross(h):
        return pltpu.make_async_remote_copy(
            rows(0, 0, h), rows(1, 0, h), own_send.at[0, 2, h], own_recv.at[0, 2, h],
            device_id=pair, device_id_type=MESH_ID,
        )

    def further(row, way):
        return pltpu.make_async_remote_copy(
            rows(row, 1 + way, way), rows(row, 3, way),
            far_send.at[row, way], far_recv.at[row, way],
            device_id=side[way], device_id_type=MESH_ID,
        )

    def relay(way):
        return pltpu.make_async_remote_copy(
            rows(0, 1 + way, way), rows(1, 1 + way, way),
            own_send.at[1, way, way], own_recv.at[1, way, way],
            device_id=pair, device_id_type=MESH_ID,
        )

    def pass_on(row, way):
        hand(row, way, way).wait_recv()
        further(row, way).start()
        if RELAY and row == 0:
            relay(way).start()

    def cross_on(h):
        cross(h).wait_recv()
        for way in range(2):
            if not (RELAY and way == h):
                hand(1, way, h).start()

    order = ((0, 0, 0), (0, 1, -1), (0, 2, 1), (0, 3, 2), (1, 0, 0), (1, 1, -1), (1, 2, 1), (1, 3, 2))

    def spot(u):
        row, _, dc = order[u]
        return at(dc, row == 1)

    def tables(u):
        here = pl.ds(pl.multiple_of(spot(u) * shard, shard), shard)
        return cos_ref[here, :], sin_ref[here, :]

    def keep(u):
        return pltpu.make_async_copy(
            mine.at[u], kv_ref.at[core, depth, spot(u), near_y], mine_sem.at[u]
        )

    def y_copy(u):
        return pltpu.make_async_remote_copy(
            mine.at[u], kv_ref.at[core, depth, spot(u), near_y],
            y_send.at[u], y_recv.at[u],
            device_id=y_side, device_id_type=MESH_ID,
        )

    def z_copy(u, way, hop, own=True):
        origin = deep(-hop if way == 0 else hop)
        ref = kv_ref.at[core, origin, spot(u)]
        if u in SPLIT:
            ref = kv_ref.at[core, origin, spot(u), near_y]
        elif hop == 3:
            ref = kv_ref.at[core, origin, spot(u), way]
        source = mine.at[u] if u in SPLIT and hop == 0 and own else ref
        return pltpu.make_async_remote_copy(
            source, ref, z_send.at[way, hop, u], z_recv.at[way, hop, u],
            device_id=z_side[way], device_id_type=MESH_ID,
        )

    def z_arrival(u, way, hop):
        origin = deep(-hop - 1 if way == 0 else hop + 1)
        ref = kv_ref.at[core, origin, spot(u)]
        if u in SPLIT:
            ref = kv_ref.at[core, origin, spot(u), near_y]
        elif hop == 3:
            ref = kv_ref.at[core, origin, spot(u), way]
        return pltpu.make_async_remote_copy(
            ref, ref, z_send.at[way, hop, u], z_recv.at[way, hop, u],
            device_id=z_side[way], device_id_type=MESH_ID,
        )

    def core_copy(u, origin, y=None, source=None):
        ref = kv_ref.at[core, origin, spot(u)]
        if y is not None:
            ref = kv_ref.at[core, origin, spot(u), y]
        return pltpu.make_async_remote_copy(
            ref if source is None else source, ref, core_send, core_recv,
            device_id=core_side, device_id_type=MESH_ID,
        )

    def origin_of(stage, way):
        return deep(-stage if way == 0 else stage)

    def y_forward(u, stage, way):
        ref = kv_ref.at[core, origin_of(stage, way), spot(u), near_y]
        return pltpu.make_async_remote_copy(
            ref, ref, fwd_send.at[u, way, stage - 1], fwd_recv.at[u, way, stage - 1],
            device_id=y_side, device_id_type=MESH_ID,
        )

    def y_landed(u, stage, way):
        ref = kv_ref.at[core, origin_of(stage, way), spot(u), 1 - near_y]
        return pltpu.make_async_remote_copy(
            ref, ref, fwd_send.at[u, way, stage - 1], fwd_recv.at[u, way, stage - 1],
            device_id=y_side, device_id_type=MESH_ID,
        )

    def hops(u, stage, way):
        return stage < 3 or (stage == 3 and (u not in SPLIT or way == u % 2))

    def keys(u):
        row, place, _ = order[u]
        y = jnp.dot(tok[row, place], wkv[...], preferred_element_type=jnp.float32)
        cosine, sine = tables(u)
        mine[u, :, :HEAD] = turn(y[:, :HEAD], cosine, sine).astype(jnp.bfloat16)
        mine[u, :, HEAD:] = y[:, HEAD:].astype(jnp.bfloat16)
        keep(u).start()
        y_copy(u).start()

    def ring(u, stage, way):
        if stage == 0:
            if u not in SPLIT:
                keep(u).wait()
                y_copy(u).wait_recv()
            z_copy(u, 0, 0).start()
            z_copy(u, 1, 0).start()
            if u in SPLIT:
                core_copy(u, depth, near_y, mine.at[u]).start()
            else:
                core_copy(u, depth).start()
            return
        z_arrival(u, way, stage - 1).wait_recv()
        if hops(u, stage, way):
            z_copy(u, way, stage, False).start()
        origin = origin_of(stage, way)
        if u in SPLIT:
            y_forward(u, stage, way).start()
            core_copy(u, origin, near_y).start()
        elif stage < 4:
            core_copy(u, origin).start()
        else:
            core_copy(u, origin, way).start()

    def landed(u, stage, way):
        if stage == 0:
            y_copy(u).wait_recv()
            core_copy(u, depth, 1 - near_y).start()
        else:
            y_landed(u, stage, way).wait_recv()
            core_copy(u, origin_of(stage, way), 1 - near_y).start()

    def queries(row, part):
        wide = 2 * HEAD
        x = tok[row].reshape(4 * shard, tok.shape[-1])
        cols = slice(part * wide, (part + 1) * wide)
        y = jnp.dot(x, wq[:, cols], preferred_element_type=jnp.float32)
        for n in range(4):
            u = next(i for i, o in enumerate(order) if o[:2] == (row, n))
            cosine, sine = tables(u)
            here = pl.ds(pl.multiple_of(spot(u) * shard, shard), shard)
            for h in range(2):
                v = y[n * shard : (n + 1) * shard, h * HEAD : (h + 1) * HEAD]
                q_ref[here, part * wide + h * HEAD : part * wide + (h + 1) * HEAD] = turn(
                    v, cosine, sine
                ).astype(jnp.bfloat16)

    def project_keys(u):
        row, place, _ = order[u]
        if u == 0:
            loads[1].wait()
            loads[2].wait()
        elif place == 3:
            further(row, 0).wait_recv()
            further(row, 1).wait_recv()
        elif place:
            hand(row, place - 1, 2 - place).wait_recv()
        keys(u)

    def project_queries(row, part):
        if (row, part) == (0, 0):
            loads[3].wait()
        queries(row, part)

    loads[0].wait()
    for h in range(2):
        hand(0, 0, h).start()
        hand(0, 1, 1 - h).start()
    for h in range(2):
        cross(h).start()
    lanes = lax.broadcasted_iota(jnp.int32, (1, HEAD), 1)
    flip = jnp.where(lanes < HEAD // 2, -1.0, 1.0)

    @pl.loop(0, pos_ref.shape[0])
    def _(step):
        here = pl.ds(pl.multiple_of(step * HEAD, HEAD), HEAD)
        spread = jnp.broadcast_to(pos_ref[pl.ds(step, 1), :].astype(jnp.float32), (HEAD, HEAD))
        angles = spread.T * inv_ref[...]
        cos_ref[here, :] = jnp.cos(angles)
        sin_ref[here, :] = jnp.sin(angles) * flip

    for kind, *rest in ORDER:
        if kind == 0:
            pass_on(*rest[:2])
        elif kind == 1:
            cross_on(rest[0])
        elif kind == 2:
            project_keys(rest[0])
        elif kind == 3:
            project_queries(*rest[:2])
        elif kind == 4:
            ring(*rest)
        else:
            landed(*rest)

    for h in range(2):
        cross(h).wait_send()
        for row in range(2):
            for way in range(2):
                hand(row, way, h).wait_send()
    for row in range(2):
        for way in range(2):
            further(row, way).wait_send()
    for u in range(len(order)):
        y_copy(u).wait_send()
        if u in SPLIT:
            keep(u).wait()
        for way in range(2):
            for stage in range(4):
                if hops(u, stage, way):
                    z_copy(u, way, stage).wait_send()
            if u in SPLIT:
                for stage in range(1, 5):
                    if hops(u, stage - 1, way):
                        y_forward(u, stage, way).wait_send()
    done = kv_ref.at[core]
    pltpu.make_async_copy(done, done, core_send).wait()
    done = kv_ref.at[1 - core]
    pltpu.make_async_copy(done, done, core_recv).wait()


def gather(tokens, wq, wk, wv, positions, groups):
    shard, width = tokens.shape
    units = groups
    hbm, vmem = pl.BlockSpec(memory_space=pl.ANY), pl.BlockSpec(memory_space=pltpu.VMEM)
    dma = pltpu.SemaphoreType.DMA
    return pl.pallas_call(
        gather_kernel,
        in_specs=[hbm, hbm, hbm, hbm, vmem, vmem],
        out_specs=[vmem, hbm],
        out_shape=[
            jax.ShapeDtypeStruct((shard * groups, wq.shape[1]), jnp.bfloat16),
            jax.ShapeDtypeStruct((2, Z_RING, groups, 2, shard, 2 * HEAD), jnp.bfloat16),
        ],
        scratch_shapes=[
            pltpu.VMEM((shard * groups, HEAD), jnp.float32),
            pltpu.VMEM((shard * groups, HEAD), jnp.float32),
            pltpu.VMEM((2, RING, shard, width), jnp.bfloat16),
            pltpu.VMEM(wq.shape, jnp.bfloat16),
            pltpu.VMEM((width, 2 * HEAD), jnp.bfloat16),
            pltpu.VMEM((units, shard, 2 * HEAD), jnp.bfloat16),
            dma((4,)),
            dma((2, 3, 2)), dma((2, 3, 2)), dma((2, 2)), dma((2, 2)),
            dma((units,)), dma((units,)), dma((units,)),
            dma((2, 4, units)), dma((2, 4, units)),
            dma((units, 2, 4)), dma((units, 2, 4)),
            dma, dma,
        ],
        compiler_params=pltpu.CompilerParams(collective_id=0, has_side_effects=True),
    )(tokens, wq, wk, wv, positions.reshape(-1, HEAD), inverse_lanes())


def body(tokens, w_query, key_weight, value_weight, w_output, block_mask, positions):
    groups = lax.axis_size("grp")
    q, kv = gather(tokens, w_query, key_weight, value_weight, positions, groups)
    mixed = attend(block_mask, q, kv)
    return reduce_out(mixed, w_output, groups)


def solution(mesh):
    return jax.shard_map(
        body,
        mesh=mesh,
        in_specs=(
            P(("blk", "grp"), None),
            P(None, "grp"),
            P(None, "grp"),
            P(None, "grp"),
            P("grp", None),
            P("blk", None),
            P("blk"),
        ),
        out_specs=P(("blk", "grp"), None),
        check_vma=False,
    )
```
